1024 devices in a mesh: frame: 64 (over x, z_lo, core), head: 16 (over z_hi, y).
Axes of the slice: x: 4, y: 8, z: 16 (z_hi: 2, z_lo: 8; z = z_hi * 8 + z_lo), core: 2. Of those that a mesh axis runs over, the one named last changes fastest.
Arguments:
- queries: bfloat16 [32768, 4096], P('frame', 'head'), may hold values from -500 to 500
- keys: bfloat16 [32768, 4096], P('frame', 'head'), may hold values from -20 to 20
- values: bfloat16 [32768, 4096], P('frame', 'head'), may hold values from -6 to 6
- cotangent: bfloat16 [32768, 4096], P('frame', 'head'), may hold values from -6 to 6
- kept: int32 [64, 6], replicated, may hold values from 0 to 3
Outputs:
- attended: bfloat16 [32768, 4096], P('frame', 'head')
- grad_queries: bfloat16 [32768, 4096], P('frame', 'head')
- grad_keys: bfloat16 [32768, 4096], P('frame', 'head')
- grad_values: bfloat16 [32768, 4096], P('frame', 'head')
The draws below stay inside these ranges and needn't reach their ends.
All inputs are finite; a program needn't handle non-finite values.
Results may differ from the reference program's by a relative error of at most 0.024.
The reference program's roundings to bfloat16 on the way count: a program that leaves them out, or rounds other values in their place, can miss the bound.
Values may be sent and summed in bfloat16 or wider, within the bound.
No kernel may reach another device: no remote copies, remote signals or barrier semaphores. Data moves between devices by JAX's collectives and lax.ppermute only.
A program may use at most 32 MiB of HBM per device.

```python
import math
import jax
import jax.numpy as jnp
from jax import lax

HD = 128
FT = 512
BS = 128
LEVELS = 3
HEADS = 32
FRAMES = 64
TOKENS = 32768
NB = 4
SLOTS = 6


def raw_keys(key):
    base = jax.random.fold_in(key, 101)
    drawn = jnp.clip(jax.random.normal(base, (TOKENS, HEADS * HD), jnp.float32), -5.0, 5.0)
    return drawn


def draw_keys(key, part):
    return raw_keys(key).astype(jnp.bfloat16)


def draw_queries(key, part):
    base = jax.random.fold_in(key, 202)
    drawn = jnp.clip(jax.random.normal(base, (TOKENS, HEADS * HD), jnp.float32), -5.0, 5.0)
    return drawn.astype(jnp.bfloat16)


def set_ends(values, rng, least, largest):
    place = [jax.random.randint(jax.random.fold_in(rng, axis), (), 0, length) for axis, length in enumerate(values.shape)]
    main_axis = values.shape.index(max(values.shape))
    neighbour = place[:main_axis] + [(place[main_axis] + 1) % values.shape[main_axis]] + place[main_axis + 1:]
    return values.at[tuple(place)].set(least).at[tuple(neighbour)].set(largest)


def levels(rng, dims, cuts, smallest, high):
    loudness, own = 1.0, jax.random.fold_in(rng, 6)
    for dim, shards_of in cuts:
        steps = jnp.exp(jax.random.uniform(jax.random.fold_in(own, dim), (shards_of,), jnp.float32, smallest / len(cuts), high / len(cuts)))
        loudness = loudness * jnp.repeat(steps, dims[dim] // shards_of).reshape([-1 if axis == dim else 1 for axis in range(len(dims))])
    return loudness


def noise(key, extent, scale, reach, pieces=(), held_as=jnp.bfloat16):
    factor_of = levels(key, extent, pieces, -0.22, 0.18) if pieces else 1.0
    values = jax.random.normal(key, extent, jnp.float32) * scale * factor_of
    return jnp.minimum(jnp.maximum(values, -reach), reach).astype(held_as)


def setup_inputs(seed: int = 0) -> dict:
    splits = jax.random.split(jax.random.key(seed), 6)
    return {
        "queries": draw_queries(jax.random.fold_in(splits[5], 71), 0),
        "keys": draw_keys(jax.random.fold_in(splits[5], 71), 0),
        "values": noise(splits[2], (TOKENS, HEADS * HD), 1.0, 6.0, ((0, 64), (1, 16))),
        "cotangent": noise(splits[3], (TOKENS, HEADS * HD), 1.0, 6.0, ((0, 64), (1, 16))),
        "kept": set_ends(jax.random.randint(splits[4], (FRAMES, SLOTS), 0, NB), jax.random.fold_in(splits[4], 1), 0, NB - 1).astype(jnp.int32),
    }


masked_score = -1e+30
norm_eps = 1e-06

def slot_offsets():
    result = []
    for level_idx in range(LEVELS):
        result.append(2 ** level_idx)
        result.append(-2 ** level_idx)
    return result

def normalize_all(matrix):
    framed = matrix.reshape(FRAMES, FT, HEADS * HD)

    def one_frame(rows):
        floats = rows.astype(jnp.float32)
        mean_sq = lax.optimization_barrier(jnp.mean(floats * floats, axis=1, keepdims=True))
        return (floats * lax.rsqrt(mean_sq + norm_eps)).astype(jnp.bfloat16)
    return lax.map(one_frame, framed).reshape(TOKENS, HEADS * HD)

def attend_frame(q_rows, k_rows, v_rows, d_rows, key_mask):
    factor = 1.0 / math.sqrt(HD)
    q_float = q_rows.astype(jnp.float32)
    k_float = k_rows.astype(jnp.float32)
    v_float = v_rows.astype(jnp.float32)
    d_float = d_rows.astype(jnp.float32)
    scores = jnp.einsum('qhd,khd->hqk', q_float, k_float) * factor
    scores = jnp.where(key_mask[None, None, :], scores, masked_score)
    top_score = lax.optimization_barrier(jnp.max(scores, axis=2, keepdims=True))
    weights = jnp.exp(scores - top_score)
    probs = weights / lax.optimization_barrier(jnp.sum(weights, axis=2, keepdims=True))
    probs_low = probs.astype(jnp.bfloat16)
    probs_back = probs_low.astype(jnp.float32)
    attended = jnp.einsum('hqk,khd->qhd', probs_back, v_float).astype(jnp.bfloat16)
    dprobs = jnp.einsum('qhd,khd->hqk', d_float, v_float)
    inner = lax.optimization_barrier(jnp.sum(d_float * attended.astype(jnp.float32), axis=2))
    dscores = probs * (dprobs - jnp.transpose(inner)[:, :, None])
    dscores_back = dscores.astype(jnp.bfloat16).astype(jnp.float32)
    grad_q = (factor * jnp.einsum('hqk,khd->qhd', dscores_back, k_float)).astype(jnp.bfloat16)
    grad_k = factor * jnp.einsum('hqk,qhd->khd', dscores_back, q_float)
    grad_v = jnp.einsum('hqk,qhd->khd', probs_back, d_float)
    return (attended, grad_q, grad_k, grad_v)

def reference(queries, keys, values, cotangent, kept):
    shape_four = (FRAMES, FT, HEADS, HD)
    q_normed = normalize_all(queries)
    k_normed = normalize_all(keys)
    q_four = q_normed.reshape(shape_four)
    k_four = k_normed.reshape(shape_four)
    v_four = values.reshape(shape_four)
    d_four = cotangent.reshape(shape_four)
    k_blocks = k_normed.reshape(FRAMES, NB, BS, HEADS, HD)
    v_blocks = values.reshape(FRAMES, NB, BS, HEADS, HD)
    offsets = slot_offsets()
    slot_count = len(offsets)
    frame_ids = jnp.arange(FRAMES, dtype=jnp.int32)
    targets = jnp.stack([frame_ids + offset for offset in offsets], axis=1).astype(jnp.int32)
    is_valid = (targets >= 0) & (targets < FRAMES)
    clipped = jnp.clip(targets, 0, FRAMES - 1).astype(jnp.int32)

    def one_frame(carry, frame_idx):
        acc_k, acc_v = carry
        targ = clipped[frame_idx]
        blocks = kept[frame_idx].astype(jnp.int32)
        flags = is_valid[frame_idx]
        far_k = k_blocks[targ, blocks].reshape(slot_count * BS, HEADS, HD)
        far_v = v_blocks[targ, blocks].reshape(slot_count * BS, HEADS, HD)
        all_k = jnp.concatenate([k_four[frame_idx], far_k], axis=0)
        all_v = jnp.concatenate([v_four[frame_idx], far_v], axis=0)
        key_mask = jnp.concatenate([jnp.ones((FT,), dtype=bool), jnp.repeat(flags, BS)])
        att, grad_q, grad_k, grad_v = attend_frame(q_four[frame_idx], all_k, all_v, d_four[frame_idx], key_mask)
        gate_flags = flags.astype(jnp.float32)[:, None, None, None]
        acc_k = acc_k.at[frame_idx].add(grad_k[:FT].reshape(NB, BS, HEADS, HD))
        acc_v = acc_v.at[frame_idx].add(grad_v[:FT].reshape(NB, BS, HEADS, HD))
        acc_k = acc_k.at[targ, blocks].add(grad_k[FT:].reshape(slot_count, BS, HEADS, HD) * gate_flags)
        acc_v = acc_v.at[targ, blocks].add(grad_v[FT:].reshape(slot_count, BS, HEADS, HD) * gate_flags)
        return ((acc_k, acc_v), (att, grad_q))
    start_k = jnp.zeros((FRAMES, NB, BS, HEADS, HD), jnp.float32)
    start_v = jnp.zeros((FRAMES, NB, BS, HEADS, HD), jnp.float32)
    (total_k, total_v), (att_all, grad_q_all) = lax.scan(one_frame, (start_k, start_v), frame_ids)
    flat = (TOKENS, HEADS * HD)
    return (att_all.reshape(flat), grad_q_all.reshape(flat), total_k.astype(jnp.bfloat16).reshape(flat), total_v.astype(jnp.bfloat16).reshape(flat))
```

```python
import functools
import math

import jax
import jax.numpy as jnp
from jax import lax
from jax.experimental import pallas as pl
from jax.experimental.pallas import tpu as pltpu
from jax.sharding import PartitionSpec as P

HD = 128
BS = 128
EXCHANGES = ((1, False), (4, True), (4, False), (2, True), (2, False), (1, True))

masked_score = -1e30
norm_eps = 1e-06

VMEM = pl.BlockSpec(memory_space=pltpu.VMEM)
SMEM = pl.BlockSpec(memory_space=pltpu.SMEM)


def params(mib):
    return pltpu.CompilerParams(vmem_limit_bytes=mib << 20)


def route(distance, shifted, frames):
    pairs = []
    for low in range(frames - distance):
        if ((low // distance) % 2 == 1) == shifted:
            pairs += [(low, low + distance), (low + distance, low)]
    return pairs


def partner(frame, distance, shifted):
    up = ((frame // distance) % 2 == 1) == shifted
    level = int(math.log2(distance))
    offset = jnp.where(up, distance, -distance)
    slot = jnp.where(up, 2 * level + 1, 2 * level)
    return offset, slot


def block_start(kept_ref, frame, frames, distance, shifted):
    offset, slot = partner(frame, distance, shifted)
    other = jnp.clip(frame + offset, 0, frames - 1)
    return pl.multiple_of(kept_ref[other, slot] * BS, BS)


def is_live(frame, frames, distance, shifted):
    offset, _ = partner(frame, distance, shifted)
    other = frame + offset
    return jnp.logical_and(other >= 0, other < frames)


def sums_kernel(q_ref, k_ref, out_ref):
    rows = []
    for ref in (q_ref, k_ref):
        for start in range(0, ref.shape[0], 128):
            total = jnp.zeros((128, 128), jnp.float32)
            for column in range(0, ref.shape[1], 128):
                part = ref[start : start + 128, column : column + 128].astype(jnp.float32)
                total += part * part
            rows.append(jnp.sum(total.T, axis=0, keepdims=True))
    packed = jnp.concatenate(rows, axis=0)
    for copy in range(out_ref.shape[0]):
        out_ref[copy] = packed


def norm_kernel(frames, width_all, frame_ref, kept_ref, sums_ref, q_ref, k_ref, v_ref, qn_ref, kn_ref, *block_refs):
    frame = frame_ref[0]
    width = q_ref.shape[1]
    total = sums_ref[0]
    for part in range(1, sums_ref.shape[0]):
        total += sums_ref[part]
    scale = lax.rsqrt(total / width_all + norm_eps)
    row = 0
    for ref, out in ((q_ref, qn_ref), (k_ref, kn_ref)):
        for start in range(0, ref.shape[0], 128):
            by_row = jnp.broadcast_to(scale[row : row + 1, :], (128, 128)).T
            row += 1
            for column in range(0, width, 128):
                part = ref[start : start + 128, column : column + 128].astype(jnp.float32)
                out[start : start + 128, column : column + 128] = (part * by_row).astype(jnp.bfloat16)
    for (distance, shifted), block in zip(EXCHANGES, block_refs):
        rows = pl.ds(block_start(kept_ref, frame, frames, distance, shifted), BS)
        block[:, :width] = kn_ref[rows, :]
        block[:, width:] = v_ref[rows, :]


def attend_kernel(frames, frame_ref, q_ref, k_ref, v_ref, d_ref, *refs):
    far_refs = refs[:6]
    att_ref, gq_ref, gk_ref, gv_ref = refs[6:10]
    back_refs = refs[10:16]
    k_all, v_all, p_all, s_all = refs[16:]
    frame = frame_ref[0]
    tokens, width = q_ref.shape
    factor = 1.0 / math.sqrt(HD)
    k_all[:tokens] = k_ref[...]
    v_all[:tokens] = v_ref[...]
    for slot, far in enumerate(far_refs):
        rows = slice(tokens + slot * BS, tokens + (slot + 1) * BS)
        k_all[rows] = far[:, :width]
        v_all[rows] = far[:, width:]
    live = [is_live(frame, frames, distance, shifted) for distance, shifted in EXCHANGES]
    total_keys = k_all.shape[0]
    chunk = 256
    contract_last = (((1,), (1,)), ((), ()))
    contract_first = (((0,), (0,)), ((), ()))
    f32 = jnp.float32
    column = lax.broadcasted_iota(jnp.int32, (1, total_keys), 1)
    allowed = column < tokens
    for slot, flag in enumerate(live):
        low = tokens + slot * BS
        inside = jnp.logical_and(column >= low, column < low + BS)
        allowed = jnp.logical_or(allowed, jnp.logical_and(inside, flag))
    for start in range(0, width, HD):
        head = slice(start, start + HD)
        keys, vals = k_all[:, head], v_all[:, head]
        for first in range(0, tokens, chunk):
            rows = slice(first, first + chunk)
            grads = d_ref[rows, head]
            scores = lax.dot_general(q_ref[rows, head], keys, contract_last, preferred_element_type=f32) * factor
            scores = jnp.where(allowed, scores, masked_score)
            weights = jnp.exp(scores - jnp.max(scores, axis=1, keepdims=True))
            probs = weights * (1.0 / jnp.sum(weights, axis=1, keepdims=True))
            probs_low = probs.astype(jnp.bfloat16)
            p_all[rows, :] = probs_low
            attended = jnp.dot(probs_low, vals, preferred_element_type=f32).astype(jnp.bfloat16)
            att_ref[rows, head] = attended
            inner = jnp.sum(grads.astype(f32) * attended.astype(f32), axis=1, keepdims=True)
            dprobs = lax.dot_general(grads, vals, contract_last, preferred_element_type=f32)
            dscores = (probs * (dprobs - inner)).astype(jnp.bfloat16)
            s_all[rows, :] = dscores
            grad_q = jnp.dot(dscores, keys, preferred_element_type=f32) * factor
            gq_ref[rows, head] = grad_q.astype(jnp.bfloat16)
        grad_k = lax.dot_general(s_all[...], q_ref[:, head], contract_first, preferred_element_type=f32) * factor
        grad_v = lax.dot_general(p_all[...], d_ref[:, head], contract_first, preferred_element_type=f32)
        gk_ref[:, head] = grad_k[:tokens]
        gv_ref[:, head] = grad_v[:tokens]
        for slot, back in enumerate(back_refs):
            rows = slice(tokens + slot * BS, tokens + (slot + 1) * BS)
            back[:, start : start + HD] = grad_k[rows].astype(jnp.bfloat16)
            back[:, width + start : width + start + HD] = grad_v[rows].astype(jnp.bfloat16)


def collect_kernel(frames, frame_ref, kept_ref, gk_ref, gv_ref, *refs):
    back_refs, (outk_ref, outv_ref, acc_k, acc_v) = refs[:6], refs[6:]
    frame = frame_ref[0]
    width = gk_ref.shape[1]
    acc_k[...] = gk_ref[...]
    acc_v[...] = gv_ref[...]
    for (distance, shifted), back in zip(EXCHANGES, back_refs):
        rows = pl.ds(block_start(kept_ref, frame, frames, distance, shifted), BS)

        @pl.when(is_live(frame, frames, distance, shifted))
        def _():
            acc_k[rows, :] += back[:, :width].astype(jnp.float32)
            acc_v[rows, :] += back[:, width:].astype(jnp.float32)

    outk_ref[...] = acc_k[...].astype(jnp.bfloat16)
    outv_ref[...] = acc_v[...].astype(jnp.bfloat16)


def swap(blocks, frames):
    return [
        lax.ppermute(block, "frame", route(distance, shifted, frames))
        for (distance, shifted), block in zip(EXCHANGES, blocks)
    ]


def on_device(queries, keys, values, cotangent, kept):
    frames = lax.axis_size("frame")
    heads = lax.axis_size("head")
    tokens, width = queries.shape
    frame = lax.axis_index("frame").reshape(1)
    flat = jax.ShapeDtypeStruct((tokens, width), jnp.bfloat16)
    wide = jax.ShapeDtypeStruct((tokens, width), jnp.float32)
    block = jax.ShapeDtypeStruct((BS, 2 * width), jnp.bfloat16)
    sums = pl.pallas_call(
        sums_kernel,
        out_shape=jax.ShapeDtypeStruct((heads, 2 * tokens // 128, 128), jnp.float32),
        in_specs=[VMEM] * 2,
        out_specs=VMEM,
        compiler_params=params(6),
        name="square_sums",
    )(queries, keys)
    sums = lax.all_to_all(sums, "head", 0, 0)
    q_norm, k_norm, *sent = pl.pallas_call(
        functools.partial(norm_kernel, frames, width * heads),
        out_shape=[flat, flat] + [block] * 6,
        in_specs=[SMEM] * 2 + [VMEM] * 4,
        out_specs=[VMEM] * 8,
        compiler_params=params(8),
        name="normalize",
    )(frame, kept, sums, queries, keys, values)
    far = swap(sent, frames)
    total_keys = tokens + 6 * BS
    attended, grad_q, own_k, own_v, *back = pl.pallas_call(
        functools.partial(attend_kernel, frames),
        out_shape=[flat, flat, wide, wide] + [block] * 6,
        in_specs=[SMEM] + [VMEM] * 10,
        out_specs=[VMEM] * 10,
        scratch_shapes=[
            pltpu.VMEM((total_keys, width), jnp.bfloat16),
            pltpu.VMEM((total_keys, width), jnp.bfloat16),
            pltpu.VMEM((tokens, total_keys), jnp.bfloat16),
            pltpu.VMEM((tokens, total_keys), jnp.bfloat16),
        ],
        compiler_params=params(32),
        name="attend",
    )(frame, q_norm, k_norm, values, cotangent, *far)
    back = swap(back, frames)
    grad_k, grad_v = pl.pallas_call(
        functools.partial(collect_kernel, frames),
        out_shape=[flat, flat],
        in_specs=[SMEM] * 2 + [VMEM] * 8,
        out_specs=[VMEM] * 2,
        scratch_shapes=[pltpu.VMEM((tokens, width), jnp.float32)] * 2,
        compiler_params=params(8),
        name="collect",
    )(frame, kept, own_k, own_v, *back)
    return attended, grad_q, grad_k, grad_v


def solution(mesh):
    spec = P("frame", "head")
    return jax.shard_map(
        on_device,
        mesh=mesh,
        in_specs=(spec, spec, spec, spec, P()),
        out_specs=(spec, spec, spec, spec),
        check_vma=False,
    )
```

```python
import functools
import math

import jax
import jax.numpy as jnp
from jax import lax
from jax.experimental import pallas as pl
from jax.experimental.pallas import tpu as pltpu
from jax.sharding import PartitionSpec as P

HD = 128
BS = 128
EXCHANGES = ((1, False), (4, True), (4, False), (2, True), (2, False), (1, True))
RETURN_ORDER = (1, 3, 5, 2, 4, 0)

masked_score = -1e30
norm_eps = 1e-06

VMEM = pl.BlockSpec(memory_space=pltpu.VMEM)
SMEM = pl.BlockSpec(memory_space=pltpu.SMEM)


def params(mib):
    return pltpu.CompilerParams(vmem_limit_bytes=mib << 20)


def route(distance, shifted, frames):
    pairs = []
    for low in range(frames - distance):
        if ((low // distance) % 2 == 1) == shifted:
            pairs += [(low, low + distance), (low + distance, low)]
    return pairs


def partner(frame, distance, shifted):
    up = ((frame // distance) % 2 == 1) == shifted
    level = int(math.log2(distance))
    offset = jnp.where(up, distance, -distance)
    slot = jnp.where(up, 2 * level + 1, 2 * level)
    return offset, slot


def block_start(kept_ref, frame, frames, distance, shifted):
    offset, slot = partner(frame, distance, shifted)
    other = jnp.clip(frame + offset, 0, frames - 1)
    return pl.multiple_of(kept_ref[other, slot] * BS, BS)


def is_live(frame, frames, distance, shifted):
    offset, _ = partner(frame, distance, shifted)
    other = frame + offset
    return jnp.logical_and(other >= 0, other < frames)


def via_near(frame):
    return ((frame % 2) ^ ((frame // 2) % 2)) == 1


def prepare_kernel(frames, frame_ref, kept_ref, q_ref, k_ref, v_ref, sums_ref, *block_refs):
    frame = frame_ref[0]
    width = k_ref.shape[1]
    rows = []
    for ref in (q_ref, k_ref):
        for start in range(0, ref.shape[0], 128):
            total = jnp.zeros((128, 128), jnp.float32)
            for column in range(0, width, 128):
                part = ref[start : start + 128, column : column + 128].astype(jnp.float32)
                total += part * part
            rows.append(jnp.sum(total.T, axis=0, keepdims=True))
    packed = jnp.concatenate(rows, axis=0)
    for copy in range(sums_ref.shape[0]):
        sums_ref[copy] = packed
    first = block_refs[0]
    targets = [first.at[:BS], *block_refs[1:], first.at[BS:]]
    for (distance, shifted), block in zip(EXCHANGES, targets):
        rows = pl.ds(block_start(kept_ref, frame, frames, distance, shifted), BS)
        block[:, :width] = k_ref[rows, :]
        block[:, width:] = v_ref[rows, :]


def by_row(scale):
    return jnp.broadcast_to(scale, (128, 128)).T


def scaled(block, scale):
    return (block.astype(jnp.float32) * scale).astype(jnp.bfloat16)


def norm_kernel(frames, width_all, frame_ref, kept_ref, sums_ref, q_ref, k_ref, qn_ref, kn_ref, scale_ref, scale_rows):
    frame = frame_ref[0]
    width = q_ref.shape[1]
    total = sums_ref[0]
    for part in range(1, sums_ref.shape[0]):
        total += sums_ref[part]
    scale = lax.rsqrt(total / width_all + norm_eps)
    scale_rows[...] = scale
    scale_ref[...] = jnp.zeros_like(scale_ref)
    for distance, shifted in EXCHANGES:
        offset, _ = partner(frame, distance, shifted)
        block = block_start(kept_ref, frame, frames, distance, shifted) // BS
        row = q_ref.shape[0] // BS + block

        @pl.when(is_live(frame, frames, distance, shifted))
        def _():
            scale_ref[frame + offset] = scale_rows[pl.ds(row, 1), :]

    row = 0
    for ref, out in ((q_ref, qn_ref), (k_ref, kn_ref)):
        for start in range(0, ref.shape[0], 128):
            factor = by_row(scale[row : row + 1, :])
            row += 1
            for column in range(0, width, 128):
                part = ref[start : start + 128, column : column + 128]
                out[start : start + 128, column : column + 128] = scaled(part, factor)


CONTRACT_LAST = (((1,), (1,)), ((), ()))
CONTRACT_FIRST = (((0,), (0,)), ((), ()))
FACTOR = 1.0 / math.sqrt(HD)
CHUNK = 256


def dot(left, right, dims=(((1,), (0,)), ((), ()))):
    return lax.dot_general(left, right, dims, preferred_element_type=jnp.float32)


def attend_kernel(frames, frame_ref, scale_ref, q_ref, k_ref, v_ref, d_ref, *refs):
    far_refs = refs[:5]
    att_ref, p_own, s_own, s_far, k_far = refs[5:10]
    back_refs = refs[10:16]
    v_far, p_far = refs[16:]
    frame = frame_ref[0]
    tokens, width = q_ref.shape
    f32 = jnp.float32

    def place(slot, far):
        distance, shifted = EXCHANGES[slot]
        offset, _ = partner(frame, distance, shifted)
        scale = by_row(scale_ref[jnp.clip(frame + offset, 0, frames - 1)])
        start = slot * BS
        for column in range(0, width, 128):
            part = far[:BS, column : column + 128]
            k_far[start : start + BS, column : column + 128] = scaled(part, scale)
        v_far[start : start + BS] = far[:BS, width:]

    for slot, far in enumerate(far_refs):
        place(slot, far)

    @pl.when(via_near(frame))
    def _():
        place(5, far_refs[4].at[BS:])

    @pl.when(jnp.logical_not(via_near(frame)))
    def _():
        place(5, far_refs[3].at[BS:])

    column = lax.broadcasted_iota(jnp.int32, (1, 6 * BS), 1)
    allowed = column < 0
    for slot, (distance, shifted) in enumerate(EXCHANGES):
        inside = jnp.logical_and(column >= slot * BS, column < (slot + 1) * BS)
        live = is_live(frame, frames, distance, shifted)
        allowed = jnp.logical_or(allowed, jnp.logical_and(inside, live))
    for index in range(width // HD):
        head = slice(index * HD, (index + 1) * HD)
        keys, vals = k_far[:, head], v_far[:, head]
        for first in range(0, tokens, CHUNK):
            rows = slice(first, first + CHUNK)
            grads = d_ref[rows, head]
            own = dot(q_ref[rows, head], k_ref[:, head], CONTRACT_LAST) * FACTOR
            far = jnp.where(allowed, dot(q_ref[rows, head], keys, CONTRACT_LAST) * FACTOR, masked_score)
            top = jnp.maximum(jnp.max(own, axis=1, keepdims=True), jnp.max(far, axis=1, keepdims=True))
            own = jnp.exp(own - top)
            far = jnp.exp(far - top)
            share = 1.0 / (jnp.sum(own, axis=1, keepdims=True) + jnp.sum(far, axis=1, keepdims=True))
            own = own * share
            far = far * share
            own_low = own.astype(jnp.bfloat16)
            far_low = far.astype(jnp.bfloat16)
            p_own[index, rows, :] = own_low
            p_far[rows, :] = far_low
            attended = (dot(own_low, v_ref[:, head]) + dot(far_low, vals)).astype(jnp.bfloat16)
            att_ref[rows, head] = attended
            inner = jnp.sum(grads.astype(f32) * attended.astype(f32), axis=1, keepdims=True)
            s_own[index, rows, :] = (own * (dot(grads, v_ref[:, head], CONTRACT_LAST) - inner)).astype(jnp.bfloat16)
            s_far[index, rows, :] = (far * (dot(grads, vals, CONTRACT_LAST) - inner)).astype(jnp.bfloat16)
        grad_k = dot(s_far[index], q_ref[:, head], CONTRACT_FIRST) * FACTOR
        grad_v = dot(p_far[...], d_ref[:, head], CONTRACT_FIRST)
        for slot, back in zip(RETURN_ORDER, back_refs):
            rows = slice(slot * BS, (slot + 1) * BS)
            back[:, index * HD : (index + 1) * HD] = grad_k[rows].astype(jnp.bfloat16)
            back[:, width + index * HD : width + (index + 1) * HD] = grad_v[rows].astype(jnp.bfloat16)


def rest_kernel(p_own, s_own, s_far, k_far, q_ref, k_ref, d_ref, gq_ref, gk_ref, gv_ref):
    for index in range(q_ref.shape[1] // HD):
        head = slice(index * HD, (index + 1) * HD)
        grad_q = dot(s_own[index], k_ref[:, head]) + dot(s_far[index], k_far[:, head])
        gq_ref[:, head] = (grad_q * FACTOR).astype(jnp.bfloat16)
        gk_ref[:, head] = dot(s_own[index], q_ref[:, head], CONTRACT_FIRST) * FACTOR
        gv_ref[:, head] = dot(p_own[index], d_ref[:, head], CONTRACT_FIRST)


def collect_kernel(frames, frame_ref, kept_ref, gk_ref, gv_ref, *refs):
    back_refs, (outk_ref, outv_ref, acc_k, acc_v) = refs[:6], refs[6:]
    frame = frame_ref[0]
    width = gk_ref.shape[1]
    acc_k[...] = gk_ref[...]
    acc_v[...] = gv_ref[...]
    for which, back in zip(RETURN_ORDER, back_refs):
        distance, shifted = EXCHANGES[which]
        rows = pl.ds(block_start(kept_ref, frame, frames, distance, shifted), BS)

        @pl.when(is_live(frame, frames, distance, shifted))
        def _():
            acc_k[rows, :] += back[:, :width].astype(jnp.float32)
            acc_v[rows, :] += back[:, width:].astype(jnp.float32)

    outk_ref[...] = acc_k[...].astype(jnp.bfloat16)
    outv_ref[...] = acc_v[...].astype(jnp.bfloat16)


def exchange(block, frames, which):
    return lax.ppermute(block, "frame", route(*EXCHANGES[which], frames))


def swap_relayed(blocks, frames):
    first, wide_far, near_far, wide_two, near_two = blocks
    got_first = exchange(first, frames, 0)
    got_wide_far = exchange(wide_far, frames, 1)
    got_near_far = exchange(near_far, frames, 2)
    relay = got_first[BS:]
    got_wide_two = exchange(jnp.concatenate([wide_two, relay]), frames, 3)
    got_near_two = exchange(jnp.concatenate([near_two, relay]), frames, 4)
    return got_first, got_wide_far, got_near_far, got_wide_two, got_near_two


def swap(blocks, frames):
    return [exchange(block, frames, which) for which, block in zip(RETURN_ORDER, blocks)]


def on_device(queries, keys, values, cotangent, kept):
    frames = lax.axis_size("frame")
    heads = lax.axis_size("head")
    tokens, width = queries.shape
    frame = lax.axis_index("frame").reshape(1)
    stat_rows = 2 * tokens // 128
    flat = jax.ShapeDtypeStruct((tokens, width), jnp.bfloat16)
    wide = jax.ShapeDtypeStruct((tokens, width), jnp.float32)
    block = jax.ShapeDtypeStruct((BS, 2 * width), jnp.bfloat16)
    pair = jax.ShapeDtypeStruct((2 * BS, 2 * width), jnp.bfloat16)
    sums, *sent = pl.pallas_call(
        functools.partial(prepare_kernel, frames),
        out_shape=[jax.ShapeDtypeStruct((heads, stat_rows, 128), jnp.float32), pair] + [block] * 4,
        in_specs=[SMEM] * 2 + [VMEM] * 3,
        out_specs=[VMEM] * 6,
        compiler_params=params(8),
        name="prepare",
    )(frame, kept, queries, keys, values)
    sums = lax.all_to_all(sums, "head", 0, 0)
    far = swap_relayed(sent, frames)
    q_norm, k_norm, scales = pl.pallas_call(
        functools.partial(norm_kernel, frames, width * heads),
        out_shape=[flat, flat, jax.ShapeDtypeStruct((frames, 1, BS), jnp.float32)],
        in_specs=[SMEM] * 2 + [VMEM] * 3,
        out_specs=[VMEM] * 3,
        scratch_shapes=[pltpu.VMEM((stat_rows, 128), jnp.float32)],
        compiler_params=params(8),
        name="normalize",
    )(frame, kept, sums, queries, keys)
    scales = lax.all_to_all(scales, "frame", 0, 0)
    heads_dev = width // HD
    own_shape = (heads_dev, tokens, tokens)
    own_flops = 2 * tokens * tokens * width
    attended, own_p, own_s, far_s, far_k, *back = pl.pallas_call(
        functools.partial(attend_kernel, frames),
        out_shape=[
            flat,
            jax.ShapeDtypeStruct(own_shape, jnp.bfloat16),
            jax.ShapeDtypeStruct(own_shape, jnp.bfloat16),
            jax.ShapeDtypeStruct((heads_dev, tokens, 6 * BS), jnp.bfloat16),
            jax.ShapeDtypeStruct((6 * BS, width), jnp.bfloat16),
        ]
        + [block] * 6,
        in_specs=[SMEM] + [VMEM] * 10,
        out_specs=[VMEM] * 11,
        scratch_shapes=[
            pltpu.VMEM((6 * BS, width), jnp.bfloat16),
            pltpu.VMEM((tokens, 6 * BS), jnp.bfloat16),
        ],
        compiler_params=params(20),
        name="attend",
    )(frame, scales, q_norm, k_norm, values, cotangent, *far)
    grad_q, own_k, own_v = pl.pallas_call(
        rest_kernel,
        out_shape=[flat, wide, wide],
        in_specs=[VMEM] * 7,
        out_specs=[VMEM] * 3,
        compiler_params=params(8),
        cost_estimate=pl.CostEstimate(flops=4 * own_flops, bytes_accessed=8 << 20, transcendentals=0),
        name="rest",
    )(own_p, own_s, far_s, far_k, q_norm, k_norm, cotangent)
    back = swap(back, frames)
    grad_k, grad_v = pl.pallas_call(
        functools.partial(collect_kernel, frames),
        out_shape=[flat, flat],
        in_specs=[SMEM] * 2 + [VMEM] * 8,
        out_specs=[VMEM] * 2,
        scratch_shapes=[pltpu.VMEM((tokens, width), jnp.float32)] * 2,
        compiler_params=params(8),
        name="collect",
    )(frame, kept, own_k, own_v, *back)
    return attended, grad_q, grad_k, grad_v


def solution(mesh):
    spec = P("frame", "head")
    return jax.shard_map(
        on_device,
        mesh=mesh,
        in_specs=(spec, spec, spec, spec, P()),
        out_specs=(spec, spec, spec, spec),
        check_vma=False,
    )
```

```python
import functools
import math

import jax
import jax.numpy as jnp
from jax import lax
from jax.experimental import pallas as pl
from jax.experimental.pallas import tpu as pltpu
from jax.sharding import PartitionSpec as P

HD = 128
BS = 128
EXCHANGES = ((1, False), (4, True), (4, False), (2, True), (2, False), (1, True))
FAR_ORDER = (0, 4, 3, 1, 2)
RETURN_ORDER = (1, 3, 5, 2, 4, 0)
QUAD = 4
PREPARE_MIB = 60

masked_score = -1e30
norm_eps = 1e-06

VMEM = pl.BlockSpec(memory_space=pltpu.VMEM)
SMEM = pl.BlockSpec(memory_space=pltpu.SMEM)


def params(mib):
    return pltpu.CompilerParams(vmem_limit_bytes=mib << 20)


def route(distance, shifted, frames):
    pairs = []
    for low in range(frames - distance):
        if ((low // distance) % 2 == 1) == shifted:
            pairs += [(low, low + distance), (low + distance, low)]
    return pairs


def partner(frame, distance, shifted):
    up = ((frame // distance) % 2 == 1) == shifted
    level = int(math.log2(distance))
    offset = jnp.where(up, distance, -distance)
    slot = jnp.where(up, 2 * level + 1, 2 * level)
    return offset, slot


def block_start(kept_ref, frame, frames, distance, shifted):
    offset, slot = partner(frame, distance, shifted)
    other = jnp.clip(frame + offset, 0, frames - 1)
    return pl.multiple_of(kept_ref[other, slot] * BS, BS)


def is_live(frame, frames, distance, shifted):
    offset, _ = partner(frame, distance, shifted)
    other = frame + offset
    return jnp.logical_and(other >= 0, other < frames)


def via_near(frame):
    return ((frame % 2) ^ ((frame // 2) % 2)) == 1


def prepare_kernel(frames, frame_ref, kept_ref, q_hbm, k_hbm, v_hbm, sums_ref, *refs):
    block_refs, (q_ref, k_ref, v_ref, sems) = refs[:5], refs[5:]
    copies = [
        pltpu.make_async_copy(source, target, sems.at[index])
        for index, (source, target) in enumerate(((q_hbm, q_ref), (k_hbm, k_ref), (v_hbm, v_ref)))
    ]
    for copy in copies:
        copy.start()
    rows = []
    for copy, ref in zip(copies, (q_ref, k_ref)):
        copy.wait()
        for start in range(0, ref.shape[0], 128):
            total = jnp.zeros((128, 128), jnp.float32)
            for column in range(0, ref.shape[1], 128):
                part = ref[start : start + 128, column : column + 128].astype(jnp.float32)
                total += part * part
            rows.append(jnp.sum(total.T, axis=0, keepdims=True))
    packed = jnp.concatenate(rows, axis=0)
    for copy in range(sums_ref.shape[0]):
        sums_ref[copy] = packed
    copies[2].wait()
    frame = frame_ref[0]
    width = k_ref.shape[1]
    first = block_refs[0]
    targets = [first.at[:BS], *block_refs[1:], first.at[BS:]]
    for (distance, shifted), block in zip(EXCHANGES, targets):
        rows = pl.ds(block_start(kept_ref, frame, frames, distance, shifted), BS)
        block[:, :width] = k_ref[rows, :]
        block[:, width:] = v_ref[rows, :]


def by_row(scale):
    return jnp.broadcast_to(scale, (128, 128)).T


def scaled(block, scale):
    return (block.astype(jnp.float32) * scale).astype(jnp.bfloat16)


def norm_kernel(width_all, sums_ref, q_ref, k_ref, qn_ref, kn_ref, scale_ref):
    width = q_ref.shape[1]
    total = sums_ref[0]
    for part in range(1, sums_ref.shape[0]):
        total += sums_ref[part]
    scale = lax.rsqrt(total / width_all + norm_eps)
    for copy in range(scale_ref.shape[0]):
        scale_ref[copy] = scale[q_ref.shape[0] // 128 :]
    row = 0
    for ref, out in ((q_ref, qn_ref), (k_ref, kn_ref)):
        for start in range(0, ref.shape[0], 128):
            factor = by_row(scale[row : row + 1, :])
            row += 1
            for column in range(0, width, 128):
                part = ref[start : start + 128, column : column + 128]
                out[start : start + 128, column : column + 128] = scaled(part, factor)


CONTRACT_LAST = (((1,), (1,)), ((), ()))
CONTRACT_FIRST = (((0,), (0,)), ((), ()))
FACTOR = 1.0 / math.sqrt(HD)
CHUNK = 256


def dot(left, right, dims=(((1,), (0,)), ((), ()))):
    return lax.dot_general(left, right, dims, preferred_element_type=jnp.float32)


def own_kernel(q_ref, k_ref, v_ref, d_ref, scores_ref, dprobs_ref):
    for index in range(q_ref.shape[1] // HD):
        head = slice(index * HD, (index + 1) * HD)
        scores_ref[index] = dot(q_ref[:, head], k_ref[:, head], CONTRACT_LAST) * FACTOR
        dprobs_ref[index] = dot(d_ref[:, head], v_ref[:, head], CONTRACT_LAST)


def attend_kernel(frames, frame_ref, kept_ref, here_ref, near_ref, wide_ref, scores_ref, dprobs_ref, q_ref, v_ref, d_ref, *refs):
    far_refs = refs[:5]
    att_ref, p_own, s_own, s_far, k_far = refs[5:10]
    back_refs = refs[10:16]
    v_far, p_far = refs[16:]
    frame = frame_ref[0]
    tokens, width = q_ref.shape
    f32 = jnp.float32

    def place(slot, far):
        distance, shifted = EXCHANGES[slot]
        offset, slot_there = partner(frame, distance, shifted)
        other = jnp.clip(frame + offset, 0, frames - 1)
        member, block = other % QUAD, pl.ds(kept_ref[frame, slot_there ^ 1], 1)
        scale = jnp.where(
            other // QUAD == (frame ^ QUAD) // QUAD, near_ref[member, block, :], wide_ref[member, block, :]
        )
        scale = by_row(jnp.where(other // QUAD == frame // QUAD, here_ref[member, block, :], scale))
        start = slot * BS
        for column in range(0, width, 128):
            part = far[:BS, column : column + 128]
            k_far[start : start + BS, column : column + 128] = scaled(part, scale)
        v_far[start : start + BS] = far[:BS, width:]

    for slot, far in zip(FAR_ORDER, far_refs):
        place(slot, far)

    @pl.when(via_near(frame))
    def _():
        place(5, far_refs[1].at[BS:])

    @pl.when(jnp.logical_not(via_near(frame)))
    def _():
        place(5, far_refs[2].at[BS:])

    column = lax.broadcasted_iota(jnp.int32, (1, 6 * BS), 1)
    allowed = column < 0
    for slot, (distance, shifted) in enumerate(EXCHANGES):
        inside = jnp.logical_and(column >= slot * BS, column < (slot + 1) * BS)
        live = is_live(frame, frames, distance, shifted)
        allowed = jnp.logical_or(allowed, jnp.logical_and(inside, live))
    for index in range(width // HD):
        head = slice(index * HD, (index + 1) * HD)
        keys, vals = k_far[:, head], v_far[:, head]
        for first in range(0, tokens, CHUNK):
            rows = slice(first, first + CHUNK)
            grads = d_ref[rows, head]
            own = scores_ref[index, rows, :]
            far = jnp.where(allowed, dot(q_ref[rows, head], keys, CONTRACT_LAST) * FACTOR, masked_score)
            top = jnp.maximum(jnp.max(own, axis=1, keepdims=True), jnp.max(far, axis=1, keepdims=True))
            own = jnp.exp(own - top)
            far = jnp.exp(far - top)
            share = 1.0 / (jnp.sum(own, axis=1, keepdims=True) + jnp.sum(far, axis=1, keepdims=True))
            own = own * share
            far = far * share
            own_low = own.astype(jnp.bfloat16)
            far_low = far.astype(jnp.bfloat16)
            p_own[index, rows, :] = own_low
            p_far[rows, :] = far_low
            attended = (dot(own_low, v_ref[:, head]) + dot(far_low, vals)).astype(jnp.bfloat16)
            att_ref[rows, head] = attended
            inner = jnp.sum(grads.astype(f32) * attended.astype(f32), axis=1, keepdims=True)
            s_own[index, rows, :] = (own * (dprobs_ref[index, rows, :] - inner)).astype(jnp.bfloat16)
            s_far[index, rows, :] = (far * (dot(grads, vals, CONTRACT_LAST) - inner)).astype(jnp.bfloat16)
        grad_k = dot(s_far[index], q_ref[:, head], CONTRACT_FIRST) * FACTOR
        grad_v = dot(p_far[...], d_ref[:, head], CONTRACT_FIRST)
        for slot, back in zip(RETURN_ORDER, back_refs):
            rows = slice(slot * BS, (slot + 1) * BS)
            back[:, index * HD : (index + 1) * HD] = grad_k[rows].astype(jnp.bfloat16)
            back[:, width + index * HD : width + (index + 1) * HD] = grad_v[rows].astype(jnp.bfloat16)


def rest_kernel(p_own, s_own, s_far, k_far, q_ref, k_ref, d_ref, gq_ref, gk_ref, gv_ref):
    for index in range(q_ref.shape[1] // HD):
        head = slice(index * HD, (index + 1) * HD)
        grad_q = dot(s_own[index], k_ref[:, head]) + dot(s_far[index], k_far[:, head])
        gq_ref[:, head] = (grad_q * FACTOR).astype(jnp.bfloat16)
        gk_ref[:, head] = dot(s_own[index], q_ref[:, head], CONTRACT_FIRST) * FACTOR
        gv_ref[:, head] = dot(p_own[index], d_ref[:, head], CONTRACT_FIRST)


def collect_kernel(frames, frame_ref, kept_ref, gk_ref, gv_ref, *refs):
    back_refs, (outk_ref, outv_ref, acc_k, acc_v) = refs[:6], refs[6:]
    frame = frame_ref[0]
    width = gk_ref.shape[1]
    acc_k[...] = gk_ref[...]
    acc_v[...] = gv_ref[...]
    for which, back in zip(RETURN_ORDER, back_refs):
        distance, shifted = EXCHANGES[which]
        rows = pl.ds(block_start(kept_ref, frame, frames, distance, shifted), BS)

        @pl.when(is_live(frame, frames, distance, shifted))
        def _():
            acc_k[rows, :] += back[:, :width].astype(jnp.float32)
            acc_v[rows, :] += back[:, width:].astype(jnp.float32)

    outk_ref[...] = acc_k[...].astype(jnp.bfloat16)
    outv_ref[...] = acc_v[...].astype(jnp.bfloat16)


def exchange(block, frames, which):
    return lax.ppermute(block, "frame", route(*EXCHANGES[which], frames))


def swap_relayed(blocks, frames):
    first, wide_far, near_far, wide_two, near_two = blocks
    got_first = exchange(first, frames, 0)
    got_wide_far = exchange(wide_far, frames, 1)
    got_near_far = exchange(near_far, frames, 2)
    relay = got_first[BS:]
    got_wide_two = exchange(jnp.concatenate([wide_two, relay]), frames, 3)
    got_near_two = exchange(jnp.concatenate([near_two, relay]), frames, 4)
    return got_first, got_near_two, got_wide_two, got_wide_far, got_near_far


def swap(blocks, frames):
    return [exchange(block, frames, which) for which, block in zip(RETURN_ORDER, blocks)]


def on_device(queries, keys, values, cotangent, kept):
    frames = lax.axis_size("frame")
    heads = lax.axis_size("head")
    tokens, width = queries.shape
    frame = lax.axis_index("frame").reshape(1)
    stat_rows = 2 * tokens // 128
    flat = jax.ShapeDtypeStruct((tokens, width), jnp.bfloat16)
    wide = jax.ShapeDtypeStruct((tokens, width), jnp.float32)
    block = jax.ShapeDtypeStruct((BS, 2 * width), jnp.bfloat16)
    pair = jax.ShapeDtypeStruct((2 * BS, 2 * width), jnp.bfloat16)
    sums, *sent = pl.pallas_call(
        functools.partial(prepare_kernel, frames),
        out_shape=[jax.ShapeDtypeStruct((heads, stat_rows, 128), jnp.float32), pair] + [block] * 4,
        in_specs=[SMEM] * 2 + [pl.BlockSpec(memory_space=pl.ANY)] * 3,
        out_specs=[VMEM] * 6,
        scratch_shapes=[pltpu.VMEM((tokens, width), jnp.bfloat16)] * 3 + [pltpu.SemaphoreType.DMA((3,))],
        compiler_params=params(PREPARE_MIB),
        name="prepare",
    )(frame, kept, queries, keys, values)
    sums = lax.all_to_all(sums, "head", 0, 0)
    far = swap_relayed(sent, frames)
    q_norm, k_norm, scales = pl.pallas_call(
        functools.partial(norm_kernel, width * heads),
        out_shape=[flat, flat, jax.ShapeDtypeStruct((QUAD, tokens // BS, BS), jnp.float32)],
        in_specs=[VMEM] * 3,
        out_specs=[VMEM] * 3,
        compiler_params=params(8),
        name="normalize",
    )(sums, queries, keys)
    quads = [list(range(low, low + QUAD)) for low in range(0, frames, QUAD)]
    here_scales = lax.all_to_all(scales, "frame", 0, 0, axis_index_groups=quads)
    wide_scales = exchange(here_scales, frames, 1)
    near_scales = exchange(here_scales, frames, 2)
    heads_dev = width // HD
    own_shape = (heads_dev, tokens, tokens)
    own_flops = 2 * tokens * tokens * width
    own_scores, own_dprobs = pl.pallas_call(
        own_kernel,
        out_shape=[jax.ShapeDtypeStruct(own_shape, jnp.float32)] * 2,
        in_specs=[VMEM] * 4,
        out_specs=[VMEM] * 2,
        compiler_params=params(8),
        cost_estimate=pl.CostEstimate(flops=2 * own_flops, bytes_accessed=5 << 20, transcendentals=0),
        name="own_scores",
    )(q_norm, k_norm, values, cotangent)
    attended, own_p, own_s, far_s, far_k, *back = pl.pallas_call(
        functools.partial(attend_kernel, frames),
        out_shape=[
            flat,
            jax.ShapeDtypeStruct(own_shape, jnp.bfloat16),
            jax.ShapeDtypeStruct(own_shape, jnp.bfloat16),
            jax.ShapeDtypeStruct((heads_dev, tokens, 6 * BS), jnp.bfloat16),
            jax.ShapeDtypeStruct((6 * BS, width), jnp.bfloat16),
        ]
        + [block] * 6,
        in_specs=[SMEM] * 2 + [VMEM] * 13,
        out_specs=[VMEM] * 11,
        scratch_shapes=[
            pltpu.VMEM((6 * BS, width), jnp.bfloat16),
            pltpu.VMEM((tokens, 6 * BS), jnp.bfloat16),
        ],
        compiler_params=params(20),
        name="attend",
    )(
        frame, kept, here_scales, near_scales, wide_scales, own_scores, own_dprobs, q_norm, values, cotangent, *far
    )
    grad_q, own_k, own_v = pl.pallas_call(
        rest_kernel,
        out_shape=[flat, wide, wide],
        in_specs=[VMEM] * 7,
        out_specs=[VMEM] * 3,
        compiler_params=params(8),
        cost_estimate=pl.CostEstimate(flops=4 * own_flops, bytes_accessed=8 << 20, transcendentals=0),
        name="rest",
    )(own_p, own_s, far_s, far_k, q_norm, k_norm, cotangent)
    back = swap(back, frames)
    grad_k, grad_v = pl.pallas_call(
        functools.partial(collect_kernel, frames),
        out_shape=[flat, flat],
        in_specs=[SMEM] * 2 + [VMEM] * 8,
        out_specs=[VMEM] * 2,
        scratch_shapes=[pltpu.VMEM((tokens, width), jnp.float32)] * 2,
        compiler_params=params(8),
        name="collect",
    )(frame, kept, own_k, own_v, *back)
    return attended, grad_q, grad_k, grad_v


def solution(mesh):
    spec = P("frame", "head")
    return jax.shard_map(
        on_device,
        mesh=mesh,
        in_specs=(spec, spec, spec, spec, P()),
        out_specs=(spec, spec, spec, spec),
        check_vma=False,
    )
```

```python
import functools
import math

import jax
import jax.numpy as jnp
from jax import lax
from jax.experimental import pallas as pl
from jax.experimental.pallas import tpu as pltpu
from jax.sharding import PartitionSpec as P

HD = 128
BS = 128
EXCHANGES = ((4, True), (2, True), (1, True), (4, False), (2, False), (1, False))
EARLY = (0, 3)

masked_score = -1e30
norm_eps = 1e-06

VMEM = pl.BlockSpec(memory_space=pltpu.VMEM)
SMEM = pl.BlockSpec(memory_space=pltpu.SMEM)


def params(mib):
    return pltpu.CompilerParams(vmem_limit_bytes=mib << 20)


def route(distance, shifted, frames):
    pairs = []
    for low in range(frames - distance):
        if ((low // distance) % 2 == 1) == shifted:
            pairs += [(low, low + distance), (low + distance, low)]
    return pairs


def partner(frame, distance, shifted):
    up = ((frame // distance) % 2 == 1) == shifted
    level = int(math.log2(distance))
    offset = jnp.where(up, distance, -distance)
    slot = jnp.where(up, 2 * level + 1, 2 * level)
    return offset, slot


def block_start(kept_ref, frame, frames, distance, shifted):
    offset, slot = partner(frame, distance, shifted)
    other = jnp.clip(frame + offset, 0, frames - 1)
    return pl.multiple_of(kept_ref[other, slot] * BS, BS)


def is_live(frame, frames, distance, shifted):
    offset, _ = partner(frame, distance, shifted)
    other = frame + offset
    return jnp.logical_and(other >= 0, other < frames)


def sums_kernel(q_ref, k_ref, sums_ref, q_held, k_held):
    rows = []
    for ref, held in ((q_ref, q_held), (k_ref, k_held)):
        for start in range(0, ref.shape[0], 128):
            total = jnp.zeros((128, 128), jnp.float32)
            for column in range(0, ref.shape[1], 128):
                part = ref[start : start + 128, column : column + 128]
                held[start : start + 128, column : column + 128] = part
                part = part.astype(jnp.float32)
                total += part * part
            rows.append(jnp.sum(total.T, axis=0, keepdims=True))
    packed = jnp.concatenate(rows, axis=0)
    for copy in range(sums_ref.shape[0]):
        sums_ref[copy] = packed


def early_kernel(frames, frame_ref, kept_ref, v_ref, v_held, *block_refs):
    v_held[...] = v_ref[...]
    for which, block in zip(EARLY, block_refs):
        block[...] = v_ref[pl.ds(block_start(kept_ref, frame_ref[0], frames, *EXCHANGES[which]), BS), :]


def by_row(scale):
    return jnp.broadcast_to(scale, (128, 128)).T


def scaled(block, scale):
    return (block.astype(jnp.float32) * scale).astype(jnp.bfloat16)


def norm_kernel(frames, width_all, frame_ref, kept_ref, sums_ref, q_ref, k_ref, v_ref, qn_ref, kn_ref, *block_refs):
    width = q_ref.shape[1]
    total = sums_ref[0]
    for part in range(1, sums_ref.shape[0]):
        total += sums_ref[part]
    scale = lax.rsqrt(total / width_all + norm_eps)
    row = 0
    for ref, out in ((q_ref, qn_ref), (k_ref, kn_ref)):
        for start in range(0, ref.shape[0], 128):
            factor = by_row(scale[row : row + 1, :])
            row += 1
            for column in range(0, width, 128):
                part = ref[start : start + 128, column : column + 128]
                out[start : start + 128, column : column + 128] = scaled(part, factor)
    for which, block in enumerate(block_refs):
        rows = pl.ds(block_start(kept_ref, frame_ref[0], frames, *EXCHANGES[which]), BS)
        block[:, :width] = kn_ref[rows, :]
        if which not in EARLY:
            block[:, width:] = v_ref[rows, :]


CONTRACT_LAST = (((1,), (1,)), ((), ()))
CONTRACT_FIRST = (((0,), (0,)), ((), ()))
FACTOR = 1.0 / math.sqrt(HD)
EXPONENT = FACTOR * math.log2(math.e)
CHUNK = 256


def dot(left, right, dims=(((1,), (0,)), ((), ()))):
    return lax.dot_general(left, right, dims, preferred_element_type=jnp.float32)


def own_kernel(q_ref, k_ref, v_ref, d_ref, scores_ref, dprobs_ref):
    for index in range(q_ref.shape[1] // HD):
        head = slice(index * HD, (index + 1) * HD)
        scores_ref[index] = dot(q_ref[:, head], k_ref[:, head], CONTRACT_LAST)
        dprobs_ref[index] = dot(d_ref[:, head], v_ref[:, head], CONTRACT_LAST)


def attend_kernel(frames, frame_ref, scores_ref, dprobs_ref, q_ref, v_ref, d_ref, *refs):
    far_refs, early_refs = refs[:6], refs[6:8]
    att_ref, p_own, s_own, s_far, k_far = refs[8:13]
    back_refs = refs[13:19]
    v_far, p_far = refs[19:]
    frame = frame_ref[0]
    tokens, width = q_ref.shape
    f32 = jnp.float32
    column = lax.broadcasted_iota(jnp.int32, (1, 6 * BS), 1)
    allowed = column < 0
    for slot, (distance, shifted) in enumerate(EXCHANGES):
        rows = slice(slot * BS, (slot + 1) * BS)
        k_far[rows] = far_refs[slot][:, :width]
        v_far[rows] = early_refs[EARLY.index(slot)][...] if slot in EARLY else far_refs[slot][:, width:]
        inside = jnp.logical_and(column >= slot * BS, column < (slot + 1) * BS)
        live = is_live(frame, frames, distance, shifted)
        allowed = jnp.logical_or(allowed, jnp.logical_and(inside, live))
    for index in range(width // HD):
        head = slice(index * HD, (index + 1) * HD)
        keys, vals = k_far[:, head], v_far[:, head]
        for first in range(0, tokens, CHUNK):
            rows = slice(first, first + CHUNK)
            grads = d_ref[rows, head]
            own = scores_ref[index, rows, :]
            far = jnp.where(allowed, dot(q_ref[rows, head], keys, CONTRACT_LAST), masked_score)
            top = jnp.maximum(jnp.max(own, axis=1, keepdims=True), jnp.max(far, axis=1, keepdims=True))
            own = jnp.exp2((own - top) * EXPONENT)
            far = jnp.exp2((far - top) * EXPONENT)
            share = 1.0 / (jnp.sum(own, axis=1, keepdims=True) + jnp.sum(far, axis=1, keepdims=True))
            own_low = (own * share).astype(jnp.bfloat16)
            far_low = (far * share).astype(jnp.bfloat16)
            p_own[index, rows, :] = own_low
            p_far[rows, :] = far_low
            attended = (dot(own_low, v_ref[:, head]) + dot(far_low, vals)).astype(jnp.bfloat16)
            att_ref[rows, head] = attended
            inner = jnp.sum(grads.astype(f32) * attended.astype(f32), axis=1, keepdims=True)
            s_own[index, rows, :] = (own * ((dprobs_ref[index, rows, :] - inner) * share)).astype(jnp.bfloat16)
            s_far[index, rows, :] = (far * ((dot(grads, vals, CONTRACT_LAST) - inner) * share)).astype(jnp.bfloat16)
        grad_k = dot(s_far[index], q_ref[:, head], CONTRACT_FIRST) * FACTOR
        grad_v = dot(p_far[...], d_ref[:, head], CONTRACT_FIRST)
        for slot, back in enumerate(back_refs):
            rows = slice(slot * BS, (slot + 1) * BS)
            back[:, index * HD : (index + 1) * HD] = grad_k[rows].astype(jnp.bfloat16)
            back[:, width + index * HD : width + (index + 1) * HD] = grad_v[rows].astype(jnp.bfloat16)


def rest_kernel(p_own, s_own, s_far, k_far, q_ref, k_ref, d_ref, gq_ref, gk_ref, gv_ref):
    for index in range(q_ref.shape[1] // HD):
        head = slice(index * HD, (index + 1) * HD)
        grad_q = dot(s_own[index], k_ref[:, head]) + dot(s_far[index], k_far[:, head])
        gq_ref[:, head] = (grad_q * FACTOR).astype(jnp.bfloat16)
        gk_ref[:, head] = dot(s_own[index], q_ref[:, head], CONTRACT_FIRST) * FACTOR
        gv_ref[:, head] = dot(p_own[index], d_ref[:, head], CONTRACT_FIRST)


def collect_kernel(frames, frame_ref, kept_ref, gk_ref, gv_ref, *refs):
    back_refs, (outk_ref, outv_ref, acc_k, acc_v) = refs[:6], refs[6:]
    frame = frame_ref[0]
    width = gk_ref.shape[1]
    acc_k[...] = gk_ref[...]
    acc_v[...] = gv_ref[...]
    for (distance, shifted), back in zip(EXCHANGES, back_refs):
        rows = pl.ds(block_start(kept_ref, frame, frames, distance, shifted), BS)

        @pl.when(is_live(frame, frames, distance, shifted))
        def _():
            acc_k[rows, :] += back[:, :width].astype(jnp.float32)
            acc_v[rows, :] += back[:, width:].astype(jnp.float32)

    outk_ref[...] = acc_k[...].astype(jnp.bfloat16)
    outv_ref[...] = acc_v[...].astype(jnp.bfloat16)


def exchange(block, frames, which):
    return lax.ppermute(block, "frame", route(*EXCHANGES[which], frames))


def on_device(queries, keys, values, cotangent, kept):
    frames = lax.axis_size("frame")
    heads = lax.axis_size("head")
    tokens, width = queries.shape
    heads_dev = width // HD
    frame = lax.axis_index("frame").reshape(1)
    flat = jax.ShapeDtypeStruct((tokens, width), jnp.bfloat16)
    wide = jax.ShapeDtypeStruct((tokens, width), jnp.float32)
    half = jax.ShapeDtypeStruct((BS, width), jnp.bfloat16)
    block = jax.ShapeDtypeStruct((BS, 2 * width), jnp.bfloat16)
    sent_shapes = [half if which in EARLY else block for which in range(len(EXCHANGES))]
    sums, queries, keys = pl.pallas_call(
        sums_kernel,
        out_shape=[jax.ShapeDtypeStruct((heads, 2 * tokens // 128, 128), jnp.float32)] + [flat] * 2,
        in_specs=[VMEM] * 2,
        out_specs=[VMEM] * 3,
        compiler_params=params(6),
        name="square_sums",
    )(queries, keys)
    sums = lax.all_to_all(sums, "head", 0, 0)
    values, *early = pl.pallas_call(
        functools.partial(early_kernel, frames),
        out_shape=[flat] + [half] * len(EARLY),
        in_specs=[SMEM] * 2 + [VMEM],
        out_specs=[VMEM] * (1 + len(EARLY)),
        compiler_params=params(6),
        name="early",
    )(frame, kept, values)
    early = [exchange(part, frames, which) for which, part in zip(EARLY, early)]
    q_norm, k_norm, *sent = pl.pallas_call(
        functools.partial(norm_kernel, frames, width * heads),
        out_shape=[flat, flat] + sent_shapes,
        in_specs=[SMEM] * 2 + [VMEM] * 4,
        out_specs=[VMEM] * 8,
        compiler_params=params(8),
        name="normalize",
    )(frame, kept, sums, queries, keys, values)
    far = [exchange(part, frames, which) for which, part in enumerate(sent)]
    own_shape = (heads_dev, tokens, tokens)
    own_flops = 2 * tokens * tokens * width
    own_scores, own_dprobs = pl.pallas_call(
        own_kernel,
        out_shape=[jax.ShapeDtypeStruct(own_shape, jnp.float32)] * 2,
        in_specs=[VMEM] * 4,
        out_specs=[VMEM] * 2,
        compiler_params=params(8),
        cost_estimate=pl.CostEstimate(flops=2 * own_flops, bytes_accessed=5 << 20, transcendentals=0),
        name="own_scores",
    )(q_norm, k_norm, values, cotangent)
    attended, own_p, own_s, far_s, far_k, *back = pl.pallas_call(
        functools.partial(attend_kernel, frames),
        out_shape=[
            flat,
            jax.ShapeDtypeStruct(own_shape, jnp.bfloat16),
            jax.ShapeDtypeStruct(own_shape, jnp.bfloat16),
            jax.ShapeDtypeStruct((heads_dev, tokens, 6 * BS), jnp.bfloat16),
            jax.ShapeDtypeStruct((6 * BS, width), jnp.bfloat16),
        ]
        + [block] * 6,
        in_specs=[SMEM] + [VMEM] * 13,
        out_specs=[VMEM] * 11,
        scratch_shapes=[
            pltpu.VMEM((6 * BS, width), jnp.bfloat16),
            pltpu.VMEM((tokens, 6 * BS), jnp.bfloat16),
        ],
        compiler_params=params(20),
        name="attend",
    )(frame, own_scores, own_dprobs, q_norm, values, cotangent, *far, *early)
    grad_q, own_k, own_v = pl.pallas_call(
        rest_kernel,
        out_shape=[flat, wide, wide],
        in_specs=[VMEM] * 7,
        out_specs=[VMEM] * 3,
        compiler_params=params(8),
        cost_estimate=pl.CostEstimate(flops=4 * own_flops, bytes_accessed=8 << 20, transcendentals=0),
        name="rest",
    )(own_p, own_s, far_s, far_k, q_norm, k_norm, cotangent)
    back = [exchange(part, frames, which) for which, part in enumerate(back)]
    grad_k, grad_v = pl.pallas_call(
        functools.partial(collect_kernel, frames),
        out_shape=[flat, flat],
        in_specs=[SMEM] * 2 + [VMEM] * 8,
        out_specs=[VMEM] * 2,
        scratch_shapes=[pltpu.VMEM((tokens, width), jnp.float32)] * 2,
        compiler_params=params(8),
        name="collect",
    )(frame, kept, own_k, own_v, *back)
    return attended, grad_q, grad_k, grad_v


def solution(mesh):
    spec = P("frame", "head")
    return jax.shard_map(
        on_device,
        mesh=mesh,
        in_specs=(spec, spec, spec, spec, P()),
        out_specs=(spec, spec, spec, spec),
        check_vma=False,
    )
```

```python
import functools
import math

import jax
import jax.numpy as jnp
from jax import lax
from jax.experimental import pallas as pl
from jax.experimental.pallas import tpu as pltpu
from jax.sharding import PartitionSpec as P

HD = 128
BS = 128
EXCHANGES = ((4, True), (2, True), (1, True), (4, False), (2, False), (1, False))

masked_score = -1e30
norm_eps = 1e-06

VMEM = pl.BlockSpec(memory_space=pltpu.VMEM)
ANY = pl.BlockSpec(memory_space=pl.ANY)
SMEM = pl.BlockSpec(memory_space=pltpu.SMEM)


def params(mib):
    return pltpu.CompilerParams(vmem_limit_bytes=mib << 20)


def route(distance, shifted, frames):
    pairs = []
    for low in range(frames - distance):
        if ((low // distance) % 2 == 1) == shifted:
            pairs += [(low, low + distance), (low + distance, low)]
    return pairs


def partner(frame, distance, shifted):
    up = ((frame // distance) % 2 == 1) == shifted
    level = int(math.log2(distance))
    offset = jnp.where(up, distance, -distance)
    slot = jnp.where(up, 2 * level + 1, 2 * level)
    return offset, slot


def block_start(kept_ref, frame, frames, distance, shifted):
    offset, slot = partner(frame, distance, shifted)
    other = jnp.clip(frame + offset, 0, frames - 1)
    return pl.multiple_of(kept_ref[slot, other] * BS, BS)


def is_live(frame, frames, distance, shifted):
    offset, _ = partner(frame, distance, shifted)
    other = frame + offset
    return jnp.logical_and(other >= 0, other < frames)


def pack_kernel(frames, frame_ref, kept_ref, k_hbm, v_hbm, *refs):
    block_refs, sems = refs[:-1], refs[-1]
    width = k_hbm.shape[1]
    copies = []
    for index, (exchange, block) in enumerate(zip(EXCHANGES, block_refs)):
        rows = pl.ds(block_start(kept_ref, frame_ref[0], frames, *exchange), BS)
        copies.append(pltpu.make_async_copy(k_hbm.at[rows, :], block.at[:, pl.ds(0, width)], sems.at[0, index]))
        copies.append(pltpu.make_async_copy(v_hbm.at[rows, :], block.at[:, pl.ds(width, width)], sems.at[1, index]))
    for copy in copies:
        copy.start()
    for copy in copies:
        copy.wait()


def square_sums(ref, start, width):
    total = jnp.zeros((128, 128), jnp.float32)
    for column in range(0, width, 128):
        part = ref[start : start + 128, column : column + 128].astype(jnp.float32)
        total += part * part
    return jnp.sum(total.T, axis=0, keepdims=True)


def own_sums_kernel(q_ref, k_ref, sums_ref):
    rows = [square_sums(ref, start, ref.shape[1]) for ref in (q_ref, k_ref) for start in range(0, ref.shape[0], 128)]
    sums_ref[...] = jnp.concatenate(rows, axis=0)


def all_sums_kernel(own_ref, *refs):
    far_refs, sums_ref = refs[:-1], refs[-1]
    rows = [own_ref[...]] + [square_sums(far, 0, far.shape[1] // 2) for far in far_refs]
    packed = jnp.concatenate(rows, axis=0)
    pad = sums_ref.shape[1] - packed.shape[0]
    packed = jnp.concatenate([packed, jnp.zeros((pad, 128), jnp.float32)], axis=0)
    for copy in range(sums_ref.shape[0]):
        sums_ref[copy] = packed


def by_row(scale):
    return jnp.broadcast_to(scale, (128, 128)).T


def scaled(block, scale):
    return (block.astype(jnp.float32) * scale).astype(jnp.bfloat16)


def norm_kernel(width_all, sums_ref, q_ref, k_ref, *refs):
    far_refs, (qn_ref, kn_ref, far_ref) = refs[:6], refs[6:]
    width = q_ref.shape[1]
    total = sums_ref[0]
    for part in range(1, sums_ref.shape[0]):
        total += sums_ref[part]
    scale = lax.rsqrt(total / width_all + norm_eps)
    pieces = [(ref, start, out, start) for ref, out in ((q_ref, qn_ref), (k_ref, kn_ref)) for start in range(0, ref.shape[0], 128)]
    pieces += [(far, 0, far_ref, slot * BS) for slot, far in enumerate(far_refs)]
    for row, (ref, start, out, place) in enumerate(pieces):
        factor = by_row(scale[row : row + 1, :])
        for column in range(0, width, 128):
            part = ref[start : start + 128, column : column + 128]
            out[place : place + 128, column : column + 128] = scaled(part, factor)


CONTRACT_LAST = (((1,), (1,)), ((), ()))
CONTRACT_FIRST = (((0,), (0,)), ((), ()))
FACTOR = 1.0 / math.sqrt(HD)
EXPONENT = FACTOR * math.log2(math.e)
CHUNK = 256


def dot(left, right, dims=(((1,), (0,)), ((), ()))):
    return lax.dot_general(left, right, dims, preferred_element_type=jnp.float32)


def attend_kernel(frames, frame_ref, q_ref, k_ref, v_ref, d_ref, k_far, *refs):
    far_refs = refs[:6]
    att_ref, p_own, s_own, s_far = refs[6:10]
    back_refs = refs[10:16]
    v_far, p_far = refs[16:]
    frame = frame_ref[0]
    tokens, width = q_ref.shape
    f32 = jnp.float32
    column = lax.broadcasted_iota(jnp.int32, (1, 6 * BS), 1)
    allowed = column < 0
    for slot, (distance, shifted) in enumerate(EXCHANGES):
        v_far[slot * BS : (slot + 1) * BS] = far_refs[slot][:, width:]
        inside = jnp.logical_and(column >= slot * BS, column < (slot + 1) * BS)
        live = is_live(frame, frames, distance, shifted)
        allowed = jnp.logical_or(allowed, jnp.logical_and(inside, live))
    for index in range(width // HD):
        head = slice(index * HD, (index + 1) * HD)
        keys, vals = k_far[:, head], v_far[:, head]
        for first in range(0, tokens, CHUNK):
            rows = slice(first, first + CHUNK)
            grads = d_ref[rows, head]
            own = dot(q_ref[rows, head], k_ref[:, head], CONTRACT_LAST)
            far = jnp.where(allowed, dot(q_ref[rows, head], keys, CONTRACT_LAST), masked_score)
            top = jnp.maximum(jnp.max(own, axis=1, keepdims=True), jnp.max(far, axis=1, keepdims=True))
            own = jnp.exp2((own - top) * EXPONENT)
            far = jnp.exp2((far - top) * EXPONENT)
            share = 1.0 / (jnp.sum(own, axis=1, keepdims=True) + jnp.sum(far, axis=1, keepdims=True))
            own_low = (own * share).astype(jnp.bfloat16)
            far_low = (far * share).astype(jnp.bfloat16)
            p_own[index, rows, :] = own_low
            p_far[rows, :] = far_low
            attended = (dot(own_low, v_ref[:, head]) + dot(far_low, vals)).astype(jnp.bfloat16)
            att_ref[rows, head] = attended
            inner = jnp.sum(grads.astype(f32) * attended.astype(f32), axis=1, keepdims=True)
            s_own[index, rows, :] = (own * ((dot(grads, v_ref[:, head], CONTRACT_LAST) - inner) * share)).astype(jnp.bfloat16)
            s_far[index, rows, :] = (far * ((dot(grads, vals, CONTRACT_LAST) - inner) * share)).astype(jnp.bfloat16)
        grad_k = dot(s_far[index], q_ref[:, head], CONTRACT_FIRST) * FACTOR
        grad_v = dot(p_far[...], d_ref[:, head], CONTRACT_FIRST)
        for slot, back in enumerate(back_refs):
            rows = slice(slot * BS, (slot + 1) * BS)
            back[:, index * HD : (index + 1) * HD] = grad_k[rows].astype(jnp.bfloat16)
            back[:, width + index * HD : width + (index + 1) * HD] = grad_v[rows].astype(jnp.bfloat16)


def rest_kernel(p_own, s_own, s_far, k_far, q_ref, k_ref, d_ref, gq_ref, gk_ref, gv_ref):
    for index in range(q_ref.shape[1] // HD):
        head = slice(index * HD, (index + 1) * HD)
        grad_q = dot(s_own[index], k_ref[:, head]) + dot(s_far[index], k_far[:, head])
        gq_ref[:, head] = (grad_q * FACTOR).astype(jnp.bfloat16)
        gk_ref[:, head] = dot(s_own[index], q_ref[:, head], CONTRACT_FIRST) * FACTOR
        gv_ref[:, head] = dot(p_own[index], d_ref[:, head], CONTRACT_FIRST)


def collect_kernel(frames, frame_ref, kept_ref, gk_ref, gv_ref, *refs):
    back_refs, (outk_ref, outv_ref, acc_k, acc_v) = refs[:6], refs[6:]
    frame = frame_ref[0]
    width = gk_ref.shape[1]
    acc_k[...] = gk_ref[...]
    acc_v[...] = gv_ref[...]
    for (distance, shifted), back in zip(EXCHANGES, back_refs):
        rows = pl.ds(block_start(kept_ref, frame, frames, distance, shifted), BS)

        @pl.when(is_live(frame, frames, distance, shifted))
        def _():
            acc_k[rows, :] += back[:, :width].astype(jnp.float32)
            acc_v[rows, :] += back[:, width:].astype(jnp.float32)

    outk_ref[...] = acc_k[...].astype(jnp.bfloat16)
    outv_ref[...] = acc_v[...].astype(jnp.bfloat16)


def exchange(block, frames, which):
    return lax.ppermute(block, "frame", route(*EXCHANGES[which], frames))


def on_device(queries, keys, values, cotangent, kept):
    frames = lax.axis_size("frame")
    heads = lax.axis_size("head")
    tokens, width = queries.shape
    heads_dev = width // HD
    frame = lax.axis_index("frame").reshape(1)
    kept = kept.T
    flat = jax.ShapeDtypeStruct((tokens, width), jnp.bfloat16)
    wide = jax.ShapeDtypeStruct((tokens, width), jnp.float32)
    block = jax.ShapeDtypeStruct((BS, 2 * width), jnp.bfloat16)
    sent = pl.pallas_call(
        functools.partial(pack_kernel, frames),
        out_shape=[block] * 6,
        in_specs=[SMEM] * 2 + [ANY] * 2,
        out_specs=[ANY] * 6,
        scratch_shapes=[pltpu.SemaphoreType.DMA((2, 6))],
        compiler_params=params(60),
        name="pack",
    )(frame, kept, keys, values)
    far = [exchange(part, frames, which) for which, part in enumerate(sent)]
    own_rows = 2 * tokens // 128
    own_sums = pl.pallas_call(
        own_sums_kernel,
        out_shape=jax.ShapeDtypeStruct((own_rows, 128), jnp.float32),
        in_specs=[VMEM] * 2,
        out_specs=VMEM,
        compiler_params=params(6),
        cost_estimate=pl.CostEstimate(flops=4 * tokens * width, bytes_accessed=4 * tokens * width, transcendentals=0),
        name="own_sums",
    )(queries, keys)
    sums = pl.pallas_call(
        all_sums_kernel,
        out_shape=jax.ShapeDtypeStruct((heads, own_rows + 8, 128), jnp.float32),
        in_specs=[VMEM] * 7,
        out_specs=VMEM,
        compiler_params=params(6),
        name="all_sums",
    )(own_sums, *far)
    sums = lax.all_to_all(sums, "head", 0, 0)
    far_shape = jax.ShapeDtypeStruct((6 * BS, width), jnp.bfloat16)
    q_norm, k_norm, far_k = pl.pallas_call(
        functools.partial(norm_kernel, width * heads),
        out_shape=[flat, flat, far_shape],
        in_specs=[VMEM] * 9,
        out_specs=[VMEM] * 3,
        compiler_params=params(8),
        name="normalize",
    )(sums, queries, keys, *far)
    own_shape = (heads_dev, tokens, tokens)
    own_flops = 2 * tokens * tokens * width
    attended, own_p, own_s, far_s, *back = pl.pallas_call(
        functools.partial(attend_kernel, frames),
        out_shape=[
            flat,
            jax.ShapeDtypeStruct(own_shape, jnp.bfloat16),
            jax.ShapeDtypeStruct(own_shape, jnp.bfloat16),
            jax.ShapeDtypeStruct((heads_dev, tokens, 6 * BS), jnp.bfloat16),
        ]
        + [block] * 6,
        in_specs=[SMEM] + [VMEM] * 11,
        out_specs=[VMEM] * 10,
        scratch_shapes=[
            pltpu.VMEM((6 * BS, width), jnp.bfloat16),
            pltpu.VMEM((tokens, 6 * BS), jnp.bfloat16),
        ],
        compiler_params=params(20),
        name="attend",
    )(frame, q_norm, k_norm, values, cotangent, far_k, *far)
    grad_q, own_k, own_v = pl.pallas_call(
        rest_kernel,
        out_shape=[flat, wide, wide],
        in_specs=[VMEM] * 7,
        out_specs=[VMEM] * 3,
        compiler_params=params(8),
        cost_estimate=pl.CostEstimate(flops=4 * own_flops, bytes_accessed=8 << 20, transcendentals=0),
        name="rest",
    )(own_p, own_s, far_s, far_k, q_norm, k_norm, cotangent)
    back = [exchange(part, frames, which) for which, part in enumerate(back)]
    grad_k, grad_v = pl.pallas_call(
        functools.partial(collect_kernel, frames),
        out_shape=[flat, flat],
        in_specs=[SMEM] * 2 + [VMEM] * 8,
        out_specs=[VMEM] * 2,
        scratch_shapes=[pltpu.VMEM((tokens, width), jnp.float32)] * 2,
        compiler_params=params(8),
        name="collect",
    )(frame, kept, own_k, own_v, *back)
    return attended, grad_q, grad_k, grad_v


def solution(mesh):
    spec = P("frame", "head")
    return jax.shard_map(
        on_device,
        mesh=mesh,
        in_specs=(spec, spec, spec, spec, P()),
        out_specs=(spec, spec, spec, spec),
        check_vma=False,
    )
```

```python
import functools
import math

import jax
import jax.numpy as jnp
from jax import lax
from jax.experimental import pallas as pl
from jax.experimental.pallas import tpu as pltpu
from jax.sharding import PartitionSpec as P

HD = 128
BS = 128
EXCHANGES = ((1, False), (4, True), (4, False), (2, True), (2, False), (1, True))
RETURN_ORDER = (1, 3, 5, 2, 4, 0)

masked_score = -1e30
norm_eps = 1e-06

VMEM = pl.BlockSpec(memory_space=pltpu.VMEM)
SMEM = pl.BlockSpec(memory_space=pltpu.SMEM)


def params(mib):
    return pltpu.CompilerParams(vmem_limit_bytes=mib << 20)


def route(distance, shifted, frames):
    pairs = []
    for low in range(frames - distance):
        if ((low // distance) % 2 == 1) == shifted:
            pairs += [(low, low + distance), (low + distance, low)]
    return pairs


def partner(frame, distance, shifted):
    up = ((frame // distance) % 2 == 1) == shifted
    level = int(math.log2(distance))
    offset = jnp.where(up, distance, -distance)
    slot = jnp.where(up, 2 * level + 1, 2 * level)
    return offset, slot


def block_start(kept_ref, frame, frames, distance, shifted):
    offset, slot = partner(frame, distance, shifted)
    other = jnp.clip(frame + offset, 0, frames - 1)
    return pl.multiple_of(kept_ref[slot, other] * BS, BS)


def is_live(frame, frames, distance, shifted):
    offset, _ = partner(frame, distance, shifted)
    other = frame + offset
    return jnp.logical_and(other >= 0, other < frames)


def via_near(frame):
    return ((frame % 2) ^ ((frame // 2) % 2)) == 1


def prepare_kernel(frames, kept_ref, q_ref, k_ref, v_ref, sums_ref, mask_ref, *block_refs):
    frame = lax.axis_index("frame")
    width = k_ref.shape[1]
    rows = []
    for ref in (q_ref, k_ref):
        for start in range(0, ref.shape[0], 128):
            total = jnp.zeros((128, 128), jnp.float32)
            for column in range(0, width, 128):
                part = ref[start : start + 128, column : column + 128].astype(jnp.float32)
                total += part * part
            rows.append(jnp.sum(total.T, axis=0, keepdims=True))
    packed = jnp.concatenate(rows, axis=0)
    for copy in range(sums_ref.shape[0]):
        sums_ref[copy] = packed
    mask_ref[...] = jnp.zeros_like(mask_ref)
    for distance, shifted in EXCHANGES:
        offset, _ = partner(frame, distance, shifted)
        block = block_start(kept_ref, frame, frames, distance, shifted) // BS

        @pl.when(is_live(frame, frames, distance, shifted))
        def _():
            mask_ref[frame + offset, pl.ds(block, 1), :] = jnp.ones((1, BS), jnp.float32)

    first = block_refs[0]
    targets = [first.at[:BS], *block_refs[1:], first.at[BS:]]
    for (distance, shifted), block in zip(EXCHANGES, targets):
        rows = pl.ds(block_start(kept_ref, frame, frames, distance, shifted), BS)
        block[:, :width] = k_ref[rows, :]
        block[:, width:] = v_ref[rows, :]


def by_row(scale):
    return jnp.broadcast_to(scale, (128, 128)).T


def scaled(block, scale):
    return (block.astype(jnp.float32) * scale).astype(jnp.bfloat16)


def norm_kernel(width_all, sums_ref, mask_ref, q_ref, k_ref, qn_ref, kn_ref, scale_ref):
    width = q_ref.shape[1]
    total = sums_ref[0]
    for part in range(1, sums_ref.shape[0]):
        total += sums_ref[part]
    scale = lax.rsqrt(total / width_all + norm_eps)
    key_scale = scale[q_ref.shape[0] // 128 :]
    for frame in range(scale_ref.shape[0]):
        scale_ref[frame] = jnp.sum(mask_ref[frame] * key_scale, axis=0, keepdims=True)
    row = 0
    for ref, out in ((q_ref, qn_ref), (k_ref, kn_ref)):
        for start in range(0, ref.shape[0], 128):
            factor = by_row(scale[row : row + 1, :])
            row += 1
            for column in range(0, width, 128):
                part = ref[start : start + 128, column : column + 128]
                out[start : start + 128, column : column + 128] = scaled(part, factor)


CONTRACT_LAST = (((1,), (1,)), ((), ()))
CONTRACT_FIRST = (((0,), (0,)), ((), ()))
FACTOR = 1.0 / math.sqrt(HD)
EXPONENT = FACTOR * math.log2(math.e)
CHUNK = 256


def dot(left, right, dims=(((1,), (0,)), ((), ()))):
    return lax.dot_general(left, right, dims, preferred_element_type=jnp.float32)


def attend_kernel(frames, scale_ref, q_ref, k_ref, v_ref, d_ref, *refs):
    far_refs = refs[:5]
    att_ref, p_own, s_own, s_far, k_far = refs[5:10]
    back_refs = refs[10:16]
    v_far, p_far = refs[16:]
    frame = lax.axis_index("frame")
    tokens, width = q_ref.shape
    f32 = jnp.float32

    def place(slot, far):
        distance, shifted = EXCHANGES[slot]
        offset, _ = partner(frame, distance, shifted)
        scale = by_row(scale_ref[jnp.clip(frame + offset, 0, frames - 1)])
        start = slot * BS
        for column in range(0, width, 128):
            part = far[:BS, column : column + 128]
            k_far[start : start + BS, column : column + 128] = scaled(part, scale)
        v_far[start : start + BS] = far[:BS, width:]

    for slot, far in enumerate(far_refs):
        place(slot, far)

    @pl.when(via_near(frame))
    def _():
        place(5, far_refs[4].at[BS:])

    @pl.when(jnp.logical_not(via_near(frame)))
    def _():
        place(5, far_refs[3].at[BS:])

    column = lax.broadcasted_iota(jnp.int32, (1, 6 * BS), 1)
    allowed = column < 0
    for slot, (distance, shifted) in enumerate(EXCHANGES):
        inside = jnp.logical_and(column >= slot * BS, column < (slot + 1) * BS)
        live = is_live(frame, frames, distance, shifted)
        allowed = jnp.logical_or(allowed, jnp.logical_and(inside, live))
    for index in range(width // HD):
        head = slice(index * HD, (index + 1) * HD)
        keys, vals = k_far[:, head], v_far[:, head]
        for first in range(0, tokens, CHUNK):
            rows = slice(first, first + CHUNK)
            grads = d_ref[rows, head]
            own = dot(q_ref[rows, head], k_ref[:, head], CONTRACT_LAST)
            far = jnp.where(allowed, dot(q_ref[rows, head], keys, CONTRACT_LAST), masked_score)
            top = jnp.maximum(jnp.max(own, axis=1, keepdims=True), jnp.max(far, axis=1, keepdims=True))
            own = jnp.exp2((own - top) * EXPONENT)
            far = jnp.exp2((far - top) * EXPONENT)
            share = 1.0 / (jnp.sum(own, axis=1, keepdims=True) + jnp.sum(far, axis=1, keepdims=True))
            own_low = (own * share).astype(jnp.bfloat16)
            far_low = (far * share).astype(jnp.bfloat16)
            p_own[index, rows, :] = own_low
            p_far[rows, :] = far_low
            attended = (dot(own_low, v_ref[:, head]) + dot(far_low, vals)).astype(jnp.bfloat16)
            att_ref[rows, head] = attended
            inner = jnp.sum(grads.astype(f32) * attended.astype(f32), axis=1, keepdims=True)
            s_own[index, rows, :] = (own * ((dot(grads, v_ref[:, head], CONTRACT_LAST) - inner) * share)).astype(jnp.bfloat16)
            s_far[index, rows, :] = (far * ((dot(grads, vals, CONTRACT_LAST) - inner) * share)).astype(jnp.bfloat16)
        grad_k = dot(s_far[index], q_ref[:, head], CONTRACT_FIRST) * FACTOR
        grad_v = dot(p_far[...], d_ref[:, head], CONTRACT_FIRST)
        for slot, back in zip(RETURN_ORDER, back_refs):
            rows = slice(slot * BS, (slot + 1) * BS)
            back[:, index * HD : (index + 1) * HD] = grad_k[rows].astype(jnp.bfloat16)
            back[:, width + index * HD : width + (index + 1) * HD] = grad_v[rows].astype(jnp.bfloat16)


def rest_kernel(p_own, s_own, s_far, k_far, q_ref, k_ref, d_ref, gq_ref, gk_ref, gv_ref):
    for index in range(q_ref.shape[1] // HD):
        head = slice(index * HD, (index + 1) * HD)
        grad_q = dot(s_own[index], k_ref[:, head]) + dot(s_far[index], k_far[:, head])
        gq_ref[:, head] = (grad_q * FACTOR).astype(jnp.bfloat16)
        gk_ref[:, head] = dot(s_own[index], q_ref[:, head], CONTRACT_FIRST) * FACTOR
        gv_ref[:, head] = dot(p_own[index], d_ref[:, head], CONTRACT_FIRST)


def collect_kernel(frames, kept_ref, gk_ref, gv_ref, *refs):
    back_refs, (outk_ref, outv_ref, acc_k, acc_v) = refs[:6], refs[6:]
    frame = lax.axis_index("frame")
    width = gk_ref.shape[1]
    acc_k[...] = gk_ref[...]
    acc_v[...] = gv_ref[...]
    for which, back in zip(RETURN_ORDER, back_refs):
        distance, shifted = EXCHANGES[which]
        rows = pl.ds(block_start(kept_ref, frame, frames, distance, shifted), BS)

        @pl.when(is_live(frame, frames, distance, shifted))
        def _():
            acc_k[rows, :] += back[:, :width].astype(jnp.float32)
            acc_v[rows, :] += back[:, width:].astype(jnp.float32)

    outk_ref[...] = acc_k[...].astype(jnp.bfloat16)
    outv_ref[...] = acc_v[...].astype(jnp.bfloat16)


def exchange(block, frames, which):
    return lax.ppermute(block, "frame", route(*EXCHANGES[which], frames))


def swap_relayed(blocks, frames):
    first, wide_far, near_far, wide_two, near_two = blocks
    got_first = exchange(first, frames, 0)
    got_wide_far = exchange(wide_far, frames, 1)
    got_near_far = exchange(near_far, frames, 2)
    relay = got_first[BS:]
    got_wide_two = exchange(jnp.concatenate([wide_two, relay]), frames, 3)
    got_near_two = exchange(jnp.concatenate([near_two, relay]), frames, 4)
    return got_first, got_wide_far, got_near_far, got_wide_two, got_near_two


def swap(blocks, frames):
    return [exchange(block, frames, which) for which, block in zip(RETURN_ORDER, blocks)]


def on_device(queries, keys, values, cotangent, kept):
    frames = lax.axis_size("frame")
    heads = lax.axis_size("head")
    tokens, width = queries.shape
    kept = kept.T
    stat_rows = 2 * tokens // 128
    flat = jax.ShapeDtypeStruct((tokens, width), jnp.bfloat16)
    wide = jax.ShapeDtypeStruct((tokens, width), jnp.float32)
    block = jax.ShapeDtypeStruct((BS, 2 * width), jnp.bfloat16)
    pair = jax.ShapeDtypeStruct((2 * BS, 2 * width), jnp.bfloat16)
    sums, mask, *sent = pl.pallas_call(
        functools.partial(prepare_kernel, frames),
        out_shape=[
            jax.ShapeDtypeStruct((heads, stat_rows, 128), jnp.float32),
            jax.ShapeDtypeStruct((frames, tokens // BS, BS), jnp.float32),
            pair,
        ]
        + [block] * 4,
        in_specs=[SMEM] + [VMEM] * 3,
        out_specs=[VMEM] * 7,
        compiler_params=params(8),
        name="prepare",
    )(kept, queries, keys, values)
    sums = lax.all_to_all(sums, "head", 0, 0)
    far = swap_relayed(sent, frames)
    q_norm, k_norm, scales = pl.pallas_call(
        functools.partial(norm_kernel, width * heads),
        out_shape=[flat, flat, jax.ShapeDtypeStruct((frames, 1, BS), jnp.float32)],
        in_specs=[VMEM] * 4,
        out_specs=[VMEM] * 3,
        compiler_params=params(8),
        name="normalize",
    )(sums, mask, queries, keys)
    scales = lax.all_to_all(scales, "frame", 0, 0)
    heads_dev = width // HD
    own_shape = (heads_dev, tokens, tokens)
    own_flops = 2 * tokens * tokens * width
    attended, own_p, own_s, far_s, far_k, *back = pl.pallas_call(
        functools.partial(attend_kernel, frames),
        out_shape=[
            flat,
            jax.ShapeDtypeStruct(own_shape, jnp.bfloat16),
            jax.ShapeDtypeStruct(own_shape, jnp.bfloat16),
            jax.ShapeDtypeStruct((heads_dev, tokens, 6 * BS), jnp.bfloat16),
            jax.ShapeDtypeStruct((6 * BS, width), jnp.bfloat16),
        ]
        + [block] * 6,
        in_specs=[VMEM] * 10,
        out_specs=[VMEM] * 11,
        scratch_shapes=[
            pltpu.VMEM((6 * BS, width), jnp.bfloat16),
            pltpu.VMEM((tokens, 6 * BS), jnp.bfloat16),
        ],
        compiler_params=params(20),
        name="attend",
    )(scales, q_norm, k_norm, values, cotangent, *far)
    grad_q, own_k, own_v = pl.pallas_call(
        rest_kernel,
        out_shape=[flat, wide, wide],
        in_specs=[VMEM] * 7,
        out_specs=[VMEM] * 3,
        compiler_params=params(8),
        cost_estimate=pl.CostEstimate(flops=4 * own_flops, bytes_accessed=8 << 20, transcendentals=0),
        name="rest",
    )(own_p, own_s, far_s, far_k, q_norm, k_norm, cotangent)
    back = swap(back, frames)
    grad_k, grad_v = pl.pallas_call(
        functools.partial(collect_kernel, frames),
        out_shape=[flat, flat],
        in_specs=[SMEM] + [VMEM] * 8,
        out_specs=[VMEM] * 2,
        scratch_shapes=[pltpu.VMEM((tokens, width), jnp.float32)] * 2,
        compiler_params=params(8),
        name="collect",
    )(kept, own_k, own_v, *back)
    return attended, grad_q, grad_k, grad_v


def solution(mesh):
    spec = P("frame", "head")
    return jax.shard_map(
        on_device,
        mesh=mesh,
        in_specs=(spec, spec, spec, spec, P()),
        out_specs=(spec, spec, spec, spec),
        check_vma=False,
    )
```

```python
import functools
import math

import jax
import jax.numpy as jnp
from jax import lax
from jax.experimental import pallas as pl
from jax.experimental.pallas import tpu as pltpu
from jax.sharding import PartitionSpec as P

HD = 128
BS = 128
EXCHANGES = ((1, False), (4, True), (4, False), (2, True), (2, False), (1, True))
RETURN_ORDER = (1, 3, 5, 2, 4, 0)

masked_score = -1e30
norm_eps = 1e-06

VMEM = pl.BlockSpec(memory_space=pltpu.VMEM)
PREPARE_MIB = 53
ANY = pl.BlockSpec(memory_space=pl.ANY)
SMEM = pl.BlockSpec(memory_space=pltpu.SMEM)


def params(mib):
    return pltpu.CompilerParams(vmem_limit_bytes=mib << 20)


def route(distance, shifted, frames):
    pairs = []
    for low in range(frames - distance):
        if ((low // distance) % 2 == 1) == shifted:
            pairs += [(low, low + distance), (low + distance, low)]
    return pairs


def partner(frame, distance, shifted):
    up = ((frame // distance) % 2 == 1) == shifted
    level = int(math.log2(distance))
    offset = jnp.where(up, distance, -distance)
    slot = jnp.where(up, 2 * level + 1, 2 * level)
    return offset, slot


def block_start(kept_ref, frame, frames, distance, shifted):
    offset, slot = partner(frame, distance, shifted)
    other = jnp.clip(frame + offset, 0, frames - 1)
    return pl.multiple_of(kept_ref[slot, other] * BS, BS)


def is_live(frame, frames, distance, shifted):
    offset, _ = partner(frame, distance, shifted)
    other = frame + offset
    return jnp.logical_and(other >= 0, other < frames)


def via_near(frame):
    return ((frame % 2) ^ ((frame // 2) % 2)) == 1


def prepare_kernel(frames, kept_ref, q_hbm, k_hbm, v_hbm, sums_ref, wanted_ref, *refs):
    block_refs, (q_ref, k_ref, v_ref, sems) = refs[:5], refs[5:]
    copies = [
        pltpu.make_async_copy(source, target, sems.at[index])
        for index, (source, target) in enumerate(((q_hbm, q_ref), (k_hbm, k_ref), (v_hbm, v_ref)))
    ]
    for copy in copies:
        copy.start()
    frame = lax.axis_index("frame")
    width = k_ref.shape[1]
    rows = []
    for copy, ref in zip(copies, (q_ref, k_ref)):
        copy.wait()
        for start in range(0, ref.shape[0], 128):
            total = jnp.zeros((128, 128), jnp.float32)
            for column in range(0, width, 128):
                part = ref[start : start + 128, column : column + 128].astype(jnp.float32)
                total += part * part
            rows.append(jnp.sum(total.T, axis=0, keepdims=True))
    packed = jnp.concatenate(rows, axis=0)
    for copy in range(sums_ref.shape[0]):
        sums_ref[copy] = packed
    wanted = []
    for distance, shifted in EXCHANGES:
        block = block_start(kept_ref, frame, frames, distance, shifted) // BS
        wanted.append(jnp.full((1, BS), block, jnp.int32))
    wanted_ref[...] = jnp.concatenate(wanted + [jnp.zeros((2, BS), jnp.int32)], axis=0)
    copies[2].wait()
    first = block_refs[0]
    targets = [first.at[:BS], *block_refs[1:], first.at[BS:]]
    for (distance, shifted), block in zip(EXCHANGES, targets):
        rows = pl.ds(block_start(kept_ref, frame, frames, distance, shifted), BS)
        block[:, :width] = k_ref[rows, :]
        block[:, width:] = v_ref[rows, :]


def by_row(scale):
    return jnp.broadcast_to(scale, (128, 128)).T


def scaled(block, scale):
    return (block.astype(jnp.float32) * scale).astype(jnp.bfloat16)


def norm_kernel(frames, width_all, sums_ref, wanted_ref, q_ref, k_ref, qn_ref, kn_ref, scale_ref):
    width = q_ref.shape[1]
    total = sums_ref[0]
    for part in range(1, sums_ref.shape[0]):
        total += sums_ref[part]
    scale = lax.rsqrt(total / width_all + norm_eps)
    key_scale = scale[q_ref.shape[0] // 128 :]
    scale_ref[...] = jnp.zeros_like(scale_ref)
    frame = lax.axis_index("frame")
    for slot, (distance, shifted) in enumerate(EXCHANGES):
        offset, _ = partner(frame, distance, shifted)
        wanted = wanted_ref[slot : slot + 1, :]
        chosen = key_scale[:1]
        for row in range(1, key_scale.shape[0]):
            chosen = jnp.where(wanted == row, key_scale[row : row + 1], chosen)

        @pl.when(is_live(frame, frames, distance, shifted))
        def _():
            scale_ref[frame + offset] = chosen

    row = 0
    for ref, out in ((q_ref, qn_ref), (k_ref, kn_ref)):
        for start in range(0, ref.shape[0], 128):
            factor = by_row(scale[row : row + 1, :])
            row += 1
            for column in range(0, width, 128):
                part = ref[start : start + 128, column : column + 128]
                out[start : start + 128, column : column + 128] = scaled(part, factor)


CONTRACT_LAST = (((1,), (1,)), ((), ()))
CONTRACT_FIRST = (((0,), (0,)), ((), ()))
FACTOR = 1.0 / math.sqrt(HD)
EXPONENT = FACTOR * math.log2(math.e)
CHUNK = 256


def dot(left, right, dims=(((1,), (0,)), ((), ()))):
    return lax.dot_general(left, right, dims, preferred_element_type=jnp.float32)


def attend_kernel(frames, scale_ref, q_ref, k_ref, v_ref, d_ref, *refs):
    far_refs = refs[:5]
    att_ref, w_own, stats, s_far, k_far = refs[5:10]
    back_refs = refs[10:16]
    v_far, p_far = refs[16:]
    frame = lax.axis_index("frame")
    tokens, width = q_ref.shape
    f32 = jnp.float32

    def place(slot, far):
        distance, shifted = EXCHANGES[slot]
        offset, _ = partner(frame, distance, shifted)
        scale = by_row(scale_ref[jnp.clip(frame + offset, 0, frames - 1)])
        start = slot * BS
        for column in range(0, width, 128):
            part = far[:BS, column : column + 128]
            k_far[start : start + BS, column : column + 128] = scaled(part, scale)
        v_far[start : start + BS] = far[:BS, width:]

    for slot, far in enumerate(far_refs):
        place(slot, far)

    @pl.when(via_near(frame))
    def _():
        place(5, far_refs[4].at[BS:])

    @pl.when(jnp.logical_not(via_near(frame)))
    def _():
        place(5, far_refs[3].at[BS:])

    column = lax.broadcasted_iota(jnp.int32, (1, 6 * BS), 1)
    allowed = column < 0
    for slot, (distance, shifted) in enumerate(EXCHANGES):
        inside = jnp.logical_and(column >= slot * BS, column < (slot + 1) * BS)
        live = is_live(frame, frames, distance, shifted)
        allowed = jnp.logical_or(allowed, jnp.logical_and(inside, live))
    for index in range(width // HD):
        head = slice(index * HD, (index + 1) * HD)
        keys, vals = k_far[:, head], v_far[:, head]
        for first in range(0, tokens, CHUNK):
            rows = slice(first, first + CHUNK)
            grads = d_ref[rows, head]
            own = dot(q_ref[rows, head], k_ref[:, head], CONTRACT_LAST)
            far = jnp.where(allowed, dot(q_ref[rows, head], keys, CONTRACT_LAST), masked_score)
            top = jnp.maximum(jnp.max(own, axis=1, keepdims=True), jnp.max(far, axis=1, keepdims=True))
            own = jnp.exp2((own - top) * EXPONENT)
            w_own[index, rows, :] = own
            far = jnp.exp2((far - top) * EXPONENT)
            share = 1.0 / (jnp.sum(own, axis=1, keepdims=True) + jnp.sum(far, axis=1, keepdims=True))
            own_low = (own * share).astype(jnp.bfloat16)
            far_low = (far * share).astype(jnp.bfloat16)
            p_far[rows, :] = far_low
            attended = (dot(own_low, v_ref[:, head]) + dot(far_low, vals)).astype(jnp.bfloat16)
            att_ref[rows, head] = attended
            inner = jnp.sum(grads.astype(f32) * attended.astype(f32), axis=1, keepdims=True)
            stats[rows, 2 * index : 2 * index + 1] = share
            stats[rows, 2 * index + 1 : 2 * index + 2] = inner
            s_far[index, rows, :] = (far * ((dot(grads, vals, CONTRACT_LAST) - inner) * share)).astype(jnp.bfloat16)
        grad_k = dot(s_far[index], q_ref[:, head], CONTRACT_FIRST) * FACTOR
        grad_v = dot(p_far[...], d_ref[:, head], CONTRACT_FIRST)
        for slot, back in zip(RETURN_ORDER, back_refs):
            rows = slice(slot * BS, (slot + 1) * BS)
            back[:, index * HD : (index + 1) * HD] = grad_k[rows].astype(jnp.bfloat16)
            back[:, width + index * HD : width + (index + 1) * HD] = grad_v[rows].astype(jnp.bfloat16)


def rest_kernel(w_own, stats, s_far, k_far, q_ref, k_ref, v_ref, d_ref, gq_ref, gk_ref, gv_ref):
    for index in range(q_ref.shape[1] // HD):
        head = slice(index * HD, (index + 1) * HD)
        share = stats[:, 2 * index : 2 * index + 1]
        inner = stats[:, 2 * index + 1 : 2 * index + 2]
        weights = w_own[index]
        probs = (weights * share).astype(jnp.bfloat16)
        dprobs = dot(d_ref[:, head], v_ref[:, head], CONTRACT_LAST)
        dscores = (weights * ((dprobs - inner) * share)).astype(jnp.bfloat16)
        grad_q = dot(dscores, k_ref[:, head]) + dot(s_far[index], k_far[:, head])
        gq_ref[:, head] = (grad_q * FACTOR).astype(jnp.bfloat16)
        gk_ref[:, head] = dot(dscores, q_ref[:, head], CONTRACT_FIRST) * FACTOR
        gv_ref[:, head] = dot(probs, d_ref[:, head], CONTRACT_FIRST)


def collect_kernel(frames, kept_ref, gk_ref, gv_ref, *refs):
    back_refs, (outk_ref, outv_ref, acc_k, acc_v) = refs[:6], refs[6:]
    frame = lax.axis_index("frame")
    width = gk_ref.shape[1]
    acc_k[...] = gk_ref[...]
    acc_v[...] = gv_ref[...]
    for which, back in zip(RETURN_ORDER, back_refs):
        distance, shifted = EXCHANGES[which]
        rows = pl.ds(block_start(kept_ref, frame, frames, distance, shifted), BS)

        @pl.when(is_live(frame, frames, distance, shifted))
        def _():
            acc_k[rows, :] += back[:, :width].astype(jnp.float32)
            acc_v[rows, :] += back[:, width:].astype(jnp.float32)

    outk_ref[...] = acc_k[...].astype(jnp.bfloat16)
    outv_ref[...] = acc_v[...].astype(jnp.bfloat16)


def exchange(block, frames, which):
    return lax.ppermute(block, "frame", route(*EXCHANGES[which], frames))


def swap_relayed(blocks, frames):
    first, wide_far, near_far, wide_two, near_two = blocks
    got_first = exchange(first, frames, 0)
    got_wide_far = exchange(wide_far, frames, 1)
    got_near_far = exchange(near_far, frames, 2)
    relay = got_first[BS:]
    got_wide_two = exchange(jnp.concatenate([wide_two, relay]), frames, 3)
    got_near_two = exchange(jnp.concatenate([near_two, relay]), frames, 4)
    return got_first, got_wide_far, got_near_far, got_wide_two, got_near_two


def swap(blocks, frames):
    return [exchange(block, frames, which) for which, block in zip(RETURN_ORDER, blocks)]


def on_device(queries, keys, values, cotangent, kept):
    frames = lax.axis_size("frame")
    heads = lax.axis_size("head")
    tokens, width = queries.shape
    kept = kept.T
    stat_rows = 2 * tokens // 128
    flat = jax.ShapeDtypeStruct((tokens, width), jnp.bfloat16)
    wide = jax.ShapeDtypeStruct((tokens, width), jnp.float32)
    block = jax.ShapeDtypeStruct((BS, 2 * width), jnp.bfloat16)
    pair = jax.ShapeDtypeStruct((2 * BS, 2 * width), jnp.bfloat16)
    sums, wanted, *sent = pl.pallas_call(
        functools.partial(prepare_kernel, frames),
        out_shape=[
            jax.ShapeDtypeStruct((heads, stat_rows, 128), jnp.float32),
            jax.ShapeDtypeStruct((8, BS), jnp.int32),
            pair,
        ]
        + [block] * 4,
        in_specs=[SMEM] + [ANY] * 3,
        out_specs=[VMEM] * 7,
        scratch_shapes=[pltpu.VMEM((tokens, width), jnp.bfloat16)] * 3 + [pltpu.SemaphoreType.DMA((3,))],
        compiler_params=params(PREPARE_MIB),
        name="prepare",
    )(kept, queries, keys, values)
    sums = lax.all_to_all(sums, "head", 0, 0)
    far = swap_relayed(sent, frames)
    q_norm, k_norm, scales = pl.pallas_call(
        functools.partial(norm_kernel, frames, width * heads),
        out_shape=[flat, flat, jax.ShapeDtypeStruct((frames, 1, BS), jnp.float32)],
        in_specs=[VMEM] * 4,
        out_specs=[VMEM] * 3,
        compiler_params=params(8),
        name="normalize",
    )(sums, wanted, queries, keys)
    scales = lax.all_to_all(scales, "frame", 0, 0)
    heads_dev = width // HD
    own_shape = (heads_dev, tokens, tokens)
    own_flops = 2 * tokens * tokens * width
    attended, own_w, stats, far_s, far_k, *back = pl.pallas_call(
        functools.partial(attend_kernel, frames),
        out_shape=[
            flat,
            jax.ShapeDtypeStruct(own_shape, jnp.float32),
            jax.ShapeDtypeStruct((tokens, 128), jnp.float32),
            jax.ShapeDtypeStruct((heads_dev, tokens, 6 * BS), jnp.bfloat16),
            jax.ShapeDtypeStruct((6 * BS, width), jnp.bfloat16),
        ]
        + [block] * 6,
        in_specs=[VMEM] * 10,
        out_specs=[VMEM] * 11,
        scratch_shapes=[
            pltpu.VMEM((6 * BS, width), jnp.bfloat16),
            pltpu.VMEM((tokens, 6 * BS), jnp.bfloat16),
        ],
        compiler_params=params(20),
        name="attend",
    )(scales, q_norm, k_norm, values, cotangent, *far)
    grad_q, own_k, own_v = pl.pallas_call(
        rest_kernel,
        out_shape=[flat, wide, wide],
        in_specs=[VMEM] * 8,
        out_specs=[VMEM] * 3,
        compiler_params=params(8),
        cost_estimate=pl.CostEstimate(flops=6 * own_flops, bytes_accessed=8 << 20, transcendentals=0),
        name="rest",
    )(own_w, stats, far_s, far_k, q_norm, k_norm, values, cotangent)
    back = swap(back, frames)
    grad_k, grad_v = pl.pallas_call(
        functools.partial(collect_kernel, frames),
        out_shape=[flat, flat],
        in_specs=[SMEM] + [VMEM] * 8,
        out_specs=[VMEM] * 2,
        scratch_shapes=[pltpu.VMEM((tokens, width), jnp.float32)] * 2,
        compiler_params=params(8),
        name="collect",
    )(kept, own_k, own_v, *back)
    return attended, grad_q, grad_k, grad_v


def solution(mesh):
    spec = P("frame", "head")
    return jax.shard_map(
        on_device,
        mesh=mesh,
        in_specs=(spec, spec, spec, spec, P()),
        out_specs=(spec, spec, spec, spec),
        check_vma=False,
    )
```

```python
import functools
import math

import jax
import jax.numpy as jnp
from jax import lax
from jax.experimental import pallas as pl
from jax.experimental.pallas import tpu as pltpu
from jax.sharding import PartitionSpec as P

HD = 128
BS = 128
EXCHANGES = ((1, False), (4, True), (4, False), (2, True), (2, False), (1, True))
RETURN_ORDER = (1, 3, 5, 2, 4, 0)

masked_score = -1e30
norm_eps = 1e-06

VMEM = pl.BlockSpec(memory_space=pltpu.VMEM)
PREPARE_MIB = 53
ANY = pl.BlockSpec(memory_space=pl.ANY)
SMEM = pl.BlockSpec(memory_space=pltpu.SMEM)


def params(mib):
    return pltpu.CompilerParams(vmem_limit_bytes=mib << 20)


def route(distance, shifted, frames):
    pairs = []
    for low in range(frames - distance):
        if ((low // distance) % 2 == 1) == shifted:
            pairs += [(low, low + distance), (low + distance, low)]
    return pairs


def partner(frame, distance, shifted):
    up = ((frame // distance) % 2 == 1) == shifted
    level = int(math.log2(distance))
    offset = jnp.where(up, distance, -distance)
    slot = jnp.where(up, 2 * level + 1, 2 * level)
    return offset, slot


def block_start(kept_ref, frame, frames, distance, shifted):
    offset, slot = partner(frame, distance, shifted)
    other = jnp.clip(frame + offset, 0, frames - 1)
    return pl.multiple_of(kept_ref[slot, other] * BS, BS)


def is_live(frame, frames, distance, shifted):
    offset, _ = partner(frame, distance, shifted)
    other = frame + offset
    return jnp.logical_and(other >= 0, other < frames)


def via_near(frame):
    return ((frame % 2) ^ ((frame // 2) % 2)) == 1


def prepare_kernel(frames, kept_ref, q_hbm, k_hbm, v_hbm, sums_ref, wanted_ref, *refs):
    block_refs, (q_ref, k_ref, v_ref, sems) = refs[:5], refs[5:]
    copies = [
        pltpu.make_async_copy(source, target, sems.at[index])
        for index, (source, target) in enumerate(((q_hbm, q_ref), (k_hbm, k_ref), (v_hbm, v_ref)))
    ]
    for copy in copies:
        copy.start()
    frame = lax.axis_index("frame")
    width = k_ref.shape[1]
    rows = []
    for copy, ref in zip(copies, (q_ref, k_ref)):
        copy.wait()
        for start in range(0, ref.shape[0], 128):
            total = jnp.zeros((128, 128), jnp.float32)
            for column in range(0, width, 128):
                part = ref[start : start + 128, column : column + 128].astype(jnp.float32)
                total += part * part
            rows.append(jnp.sum(total.T, axis=0, keepdims=True))
    packed = jnp.concatenate(rows, axis=0)
    for copy in range(sums_ref.shape[0]):
        sums_ref[copy] = packed
    wanted = []
    for distance, shifted in EXCHANGES:
        block = block_start(kept_ref, frame, frames, distance, shifted) // BS
        wanted.append(jnp.full((1, BS), block, jnp.int32))
    wanted_ref[...] = jnp.concatenate(wanted + [jnp.zeros((2, BS), jnp.int32)], axis=0)
    copies[2].wait()
    first = block_refs[0]
    targets = [first.at[:BS], *block_refs[1:], first.at[BS:]]
    for (distance, shifted), block in zip(EXCHANGES, targets):
        rows = pl.ds(block_start(kept_ref, frame, frames, distance, shifted), BS)
        block[:, :width] = k_ref[rows, :]
        block[:, width:] = v_ref[rows, :]


def by_row(scale):
    return jnp.broadcast_to(scale, (128, 128)).T


def scaled(block, scale):
    return (block.astype(jnp.float32) * scale).astype(jnp.bfloat16)


def norm_kernel(frames, width_all, sums_ref, wanted_ref, q_ref, k_ref, qn_ref, kn_ref, scale_ref):
    width = q_ref.shape[1]
    total = sums_ref[0]
    for part in range(1, sums_ref.shape[0]):
        total += sums_ref[part]
    scale = lax.rsqrt(total / width_all + norm_eps)
    key_scale = scale[q_ref.shape[0] // 128 :]
    scale_ref[...] = jnp.zeros_like(scale_ref)
    frame = lax.axis_index("frame")
    for slot, (distance, shifted) in enumerate(EXCHANGES):
        offset, _ = partner(frame, distance, shifted)
        wanted = wanted_ref[slot : slot + 1, :]
        chosen = key_scale[:1]
        for row in range(1, key_scale.shape[0]):
            chosen = jnp.where(wanted == row, key_scale[row : row + 1], chosen)

        @pl.when(is_live(frame, frames, distance, shifted))
        def _():
            scale_ref[frame + offset] = chosen

    row = 0
    for ref, out in ((q_ref, qn_ref), (k_ref, kn_ref)):
        for start in range(0, ref.shape[0], 128):
            factor = by_row(scale[row : row + 1, :])
            row += 1
            for column in range(0, width, 128):
                part = ref[start : start + 128, column : column + 128]
                out[start : start + 128, column : column + 128] = scaled(part, factor)


CONTRACT_LAST = (((1,), (1,)), ((), ()))
CONTRACT_FIRST = (((0,), (0,)), ((), ()))
FACTOR = 1.0 / math.sqrt(HD)
EXPONENT = FACTOR * math.log2(math.e)
CHUNK = 512


def dot(left, right, dims=(((1,), (0,)), ((), ()))):
    return lax.dot_general(left, right, dims, preferred_element_type=jnp.float32)


def attend_kernel(frames, scale_ref, q_ref, k_ref, v_ref, d_ref, *refs):
    far_refs = refs[:5]
    att_ref, w_own, stats, s_far, k_far = refs[5:10]
    back_refs = refs[10:16]
    v_far, p_far = refs[16:]
    frame = lax.axis_index("frame")
    tokens, width = q_ref.shape
    f32 = jnp.float32

    def place(slot, far):
        distance, shifted = EXCHANGES[slot]
        offset, _ = partner(frame, distance, shifted)
        scale = by_row(scale_ref[jnp.clip(frame + offset, 0, frames - 1)])
        start = slot * BS
        for column in range(0, width, 128):
            part = far[:BS, column : column + 128]
            k_far[start : start + BS, column : column + 128] = scaled(part, scale)
        v_far[start : start + BS] = far[:BS, width:]

    for slot, far in enumerate(far_refs):
        place(slot, far)

    @pl.when(via_near(frame))
    def _():
        place(5, far_refs[4].at[BS:])

    @pl.when(jnp.logical_not(via_near(frame)))
    def _():
        place(5, far_refs[3].at[BS:])

    column = lax.broadcasted_iota(jnp.int32, (1, 6 * BS), 1)
    allowed = column < 0
    for slot, (distance, shifted) in enumerate(EXCHANGES):
        inside = jnp.logical_and(column >= slot * BS, column < (slot + 1) * BS)
        live = is_live(frame, frames, distance, shifted)
        allowed = jnp.logical_or(allowed, jnp.logical_and(inside, live))
    for index in range(width // HD):
        head = slice(index * HD, (index + 1) * HD)
        keys, vals = k_far[:, head], v_far[:, head]
        for first in range(0, tokens, CHUNK):
            rows = slice(first, first + CHUNK)
            grads = d_ref[rows, head]
            own = dot(q_ref[rows, head], k_ref[:, head], CONTRACT_LAST)
            far = jnp.where(allowed, dot(q_ref[rows, head], keys, CONTRACT_LAST), masked_score)
            top = jnp.maximum(jnp.max(own, axis=1, keepdims=True), jnp.max(far, axis=1, keepdims=True))
            own = jnp.exp2((own - top) * EXPONENT)
            w_own[index, rows, :] = own
            far = jnp.exp2((far - top) * EXPONENT)
            share = 1.0 / (jnp.sum(own, axis=1, keepdims=True) + jnp.sum(far, axis=1, keepdims=True))
            own_low = (own * share).astype(jnp.bfloat16)
            far_low = (far * share).astype(jnp.bfloat16)
            p_far[rows, :] = far_low
            attended = (dot(own_low, v_ref[:, head]) + dot(far_low, vals)).astype(jnp.bfloat16)
            att_ref[rows, head] = attended
            inner = jnp.sum(grads.astype(f32) * attended.astype(f32), axis=1, keepdims=True)
            stats[rows, 2 * index : 2 * index + 1] = share
            stats[rows, 2 * index + 1 : 2 * index + 2] = inner
            s_far[index, rows, :] = (far * ((dot(grads, vals, CONTRACT_LAST) - inner) * share)).astype(jnp.bfloat16)
        grad_k = dot(q_ref[:, head].T, s_far[index]).T * FACTOR
        grad_v = dot(d_ref[:, head].T, p_far[...]).T
        for slot, back in zip(RETURN_ORDER, back_refs):
            rows = slice(slot * BS, (slot + 1) * BS)
            back[:, index * HD : (index + 1) * HD] = grad_k[rows].astype(jnp.bfloat16)
            back[:, width + index * HD : width + (index + 1) * HD] = grad_v[rows].astype(jnp.bfloat16)


def rest_kernel(w_own, stats, s_far, k_far, q_ref, k_ref, v_ref, d_ref, gq_ref, gk_ref, gv_ref):
    for index in range(q_ref.shape[1] // HD):
        head = slice(index * HD, (index + 1) * HD)
        share = stats[:, 2 * index : 2 * index + 1]
        inner = stats[:, 2 * index + 1 : 2 * index + 2]
        weights = w_own[index]
        probs = (weights * share).astype(jnp.bfloat16)
        dprobs = dot(d_ref[:, head], v_ref[:, head], CONTRACT_LAST)
        dscores = (weights * ((dprobs - inner) * share)).astype(jnp.bfloat16)
        grad_q = dot(dscores, k_ref[:, head]) + dot(s_far[index], k_far[:, head])
        gq_ref[:, head] = (grad_q * FACTOR).astype(jnp.bfloat16)
        gk_ref[:, head] = dot(dscores, q_ref[:, head], CONTRACT_FIRST) * FACTOR
        gv_ref[:, head] = dot(probs, d_ref[:, head], CONTRACT_FIRST)


def collect_kernel(frames, kept_ref, gk_ref, gv_ref, *refs):
    back_refs, (outk_ref, outv_ref, acc_k, acc_v) = refs[:6], refs[6:]
    frame = lax.axis_index("frame")
    width = gk_ref.shape[1]
    acc_k[...] = gk_ref[...]
    acc_v[...] = gv_ref[...]
    for which, back in zip(RETURN_ORDER, back_refs):
        distance, shifted = EXCHANGES[which]
        rows = pl.ds(block_start(kept_ref, frame, frames, distance, shifted), BS)

        @pl.when(is_live(frame, frames, distance, shifted))
        def _():
            acc_k[rows, :] += back[:, :width].astype(jnp.float32)
            acc_v[rows, :] += back[:, width:].astype(jnp.float32)

    outk_ref[...] = acc_k[...].astype(jnp.bfloat16)
    outv_ref[...] = acc_v[...].astype(jnp.bfloat16)


def exchange(block, frames, which):
    return lax.ppermute(block, "frame", route(*EXCHANGES[which], frames))


def swap_relayed(blocks, frames):
    first, wide_far, near_far, wide_two, near_two = blocks
    got_first = exchange(first, frames, 0)
    got_wide_far = exchange(wide_far, frames, 1)
    got_near_far = exchange(near_far, frames, 2)
    relay, got_near_far, got_wide_far = lax.optimization_barrier((got_first[BS:], got_near_far, got_wide_far))
    got_wide_two = exchange(jnp.concatenate([wide_two, relay]), frames, 3)
    got_near_two = exchange(jnp.concatenate([near_two, relay]), frames, 4)
    return got_first, got_wide_far, got_near_far, got_wide_two, got_near_two


def swap(blocks, frames):
    return [exchange(block, frames, which) for which, block in zip(RETURN_ORDER, blocks)]


def on_device(queries, keys, values, cotangent, kept):
    frames = lax.axis_size("frame")
    heads = lax.axis_size("head")
    tokens, width = queries.shape
    kept = kept.T
    stat_rows = 2 * tokens // 128
    flat = jax.ShapeDtypeStruct((tokens, width), jnp.bfloat16)
    wide = jax.ShapeDtypeStruct((tokens, width), jnp.float32)
    block = jax.ShapeDtypeStruct((BS, 2 * width), jnp.bfloat16)
    pair = jax.ShapeDtypeStruct((2 * BS, 2 * width), jnp.bfloat16)
    sums, wanted, *sent = pl.pallas_call(
        functools.partial(prepare_kernel, frames),
        out_shape=[
            jax.ShapeDtypeStruct((heads, stat_rows, 128), jnp.float32),
            jax.ShapeDtypeStruct((8, BS), jnp.int32),
            pair,
        ]
        + [block] * 4,
        in_specs=[SMEM] + [ANY] * 3,
        out_specs=[VMEM] * 7,
        scratch_shapes=[pltpu.VMEM((tokens, width), jnp.bfloat16)] * 3 + [pltpu.SemaphoreType.DMA((3,))],
        compiler_params=params(PREPARE_MIB),
        name="prepare",
    )(kept, queries, keys, values)
    sums = lax.all_to_all(sums, "head", 0, 0)
    far = swap_relayed(sent, frames)
    q_norm, k_norm, scales = pl.pallas_call(
        functools.partial(norm_kernel, frames, width * heads),
        out_shape=[flat, flat, jax.ShapeDtypeStruct((frames, 1, BS), jnp.float32)],
        in_specs=[VMEM] * 4,
        out_specs=[VMEM] * 3,
        compiler_params=params(8),
        name="normalize",
    )(sums, wanted, queries, keys)
    scales = lax.all_to_all(scales, "frame", 0, 0)
    heads_dev = width // HD
    own_shape = (heads_dev, tokens, tokens)
    own_flops = 2 * tokens * tokens * width
    attended, own_w, stats, far_s, far_k, *back = pl.pallas_call(
        functools.partial(attend_kernel, frames),
        out_shape=[
            flat,
            jax.ShapeDtypeStruct(own_shape, jnp.float32),
            jax.ShapeDtypeStruct((tokens, 128), jnp.float32),
            jax.ShapeDtypeStruct((heads_dev, tokens, 6 * BS), jnp.bfloat16),
            jax.ShapeDtypeStruct((6 * BS, width), jnp.bfloat16),
        ]
        + [block] * 6,
        in_specs=[VMEM] * 10,
        out_specs=[VMEM] * 11,
        scratch_shapes=[
            pltpu.VMEM((6 * BS, width), jnp.bfloat16),
            pltpu.VMEM((tokens, 6 * BS), jnp.bfloat16),
        ],
        compiler_params=params(20),
        name="attend",
    )(scales, q_norm, k_norm, values, cotangent, *far)
    grad_q, own_k, own_v = pl.pallas_call(
        rest_kernel,
        out_shape=[flat, wide, wide],
        in_specs=[VMEM] * 8,
        out_specs=[VMEM] * 3,
        compiler_params=params(8),
        cost_estimate=pl.CostEstimate(flops=6 * own_flops, bytes_accessed=8 << 20, transcendentals=0),
        name="rest",
    )(own_w, stats, far_s, far_k, q_norm, k_norm, values, cotangent)
    back = swap(back, frames)
    grad_k, grad_v = pl.pallas_call(
        functools.partial(collect_kernel, frames),
        out_shape=[flat, flat],
        in_specs=[SMEM] + [VMEM] * 8,
        out_specs=[VMEM] * 2,
        scratch_shapes=[pltpu.VMEM((tokens, width), jnp.float32)] * 2,
        compiler_params=params(8),
        name="collect",
    )(kept, own_k, own_v, *back)
    return attended, grad_q, grad_k, grad_v


def solution(mesh):
    spec = P("frame", "head")
    return jax.shard_map(
        on_device,
        mesh=mesh,
        in_specs=(spec, spec, spec, spec, P()),
        out_specs=(spec, spec, spec, spec),
        check_vma=False,
    )
```

```python
import functools
import math

import jax
import jax.numpy as jnp
from jax import lax
from jax.experimental import pallas as pl
from jax.experimental.pallas import tpu as pltpu
from jax.sharding import PartitionSpec as P

HD = 128
BS = 128
EXCHANGES = ((1, False), (4, True), (4, False), (2, True), (2, False), (1, True))
FAR_ORDER = (0, 4, 3, 1, 2)
RETURN_ORDER = (1, 3, 5, 2, 4, 0)

masked_score = -1e30
norm_eps = 1e-06

VMEM = pl.BlockSpec(memory_space=pltpu.VMEM)
PREPARE_MIB = 53
ANY = pl.BlockSpec(memory_space=pl.ANY)
SMEM = pl.BlockSpec(memory_space=pltpu.SMEM)


def params(mib):
    return pltpu.CompilerParams(vmem_limit_bytes=mib << 20)


def route(distance, shifted, frames):
    pairs = []
    for low in range(frames - distance):
        if ((low // distance) % 2 == 1) == shifted:
            pairs += [(low, low + distance), (low + distance, low)]
    return pairs


def partner(frame, distance, shifted):
    up = ((frame // distance) % 2 == 1) == shifted
    level = int(math.log2(distance))
    offset = jnp.where(up, distance, -distance)
    slot = jnp.where(up, 2 * level + 1, 2 * level)
    return offset, slot


def block_start(kept_ref, frame, frames, distance, shifted):
    offset, slot = partner(frame, distance, shifted)
    other = jnp.clip(frame + offset, 0, frames - 1)
    return pl.multiple_of(kept_ref[slot, other] * BS, BS)


def is_live(frame, frames, distance, shifted):
    offset, _ = partner(frame, distance, shifted)
    other = frame + offset
    return jnp.logical_and(other >= 0, other < frames)


def via_near(frame):
    return ((frame % 2) ^ ((frame // 2) % 2)) == 1


def prepare_kernel(frames, kept_ref, q_hbm, k_hbm, v_hbm, sums_ref, wanted_ref, *refs):
    block_refs, (q_ref, k_ref, v_ref, sems) = refs[:5], refs[5:]
    copies = [
        pltpu.make_async_copy(source, target, sems.at[index])
        for index, (source, target) in enumerate(((q_hbm, q_ref), (k_hbm, k_ref), (v_hbm, v_ref)))
    ]
    for copy in copies:
        copy.start()
    frame = lax.axis_index("frame")
    width = k_ref.shape[1]
    rows = []
    for copy, ref in zip(copies, (q_ref, k_ref)):
        copy.wait()
        for start in range(0, ref.shape[0], 128):
            total = jnp.zeros((128, 128), jnp.float32)
            for column in range(0, width, 128):
                part = ref[start : start + 128, column : column + 128].astype(jnp.float32)
                total += part * part
            rows.append(jnp.sum(total.T, axis=0, keepdims=True))
    packed = jnp.concatenate(rows, axis=0)
    for copy in range(sums_ref.shape[0]):
        sums_ref[copy] = packed
    wanted = []
    for distance, shifted in EXCHANGES:
        block = block_start(kept_ref, frame, frames, distance, shifted) // BS
        wanted.append(jnp.full((1, BS), block, jnp.int32))
    wanted_ref[...] = jnp.concatenate(wanted + [jnp.zeros((2, BS), jnp.int32)], axis=0)
    copies[2].wait()
    first = block_refs[0]
    targets = [first.at[:BS], *block_refs[1:], first.at[BS:]]
    for (distance, shifted), block in zip(EXCHANGES, targets):
        rows = pl.ds(block_start(kept_ref, frame, frames, distance, shifted), BS)
        block[:, :width] = k_ref[rows, :]
        block[:, width:] = v_ref[rows, :]


def by_row(scale):
    return jnp.broadcast_to(scale, (128, 128)).T


def scaled(block, scale):
    return (block.astype(jnp.float32) * scale).astype(jnp.bfloat16)


def norm_kernel(frames, width_all, sums_ref, wanted_ref, q_ref, k_ref, qn_ref, kn_ref, scale_ref):
    width = q_ref.shape[1]
    total = sums_ref[0]
    for part in range(1, sums_ref.shape[0]):
        total += sums_ref[part]
    scale = lax.rsqrt(total / width_all + norm_eps)
    key_scale = scale[q_ref.shape[0] // 128 :]
    scale_ref[...] = jnp.zeros_like(scale_ref)
    frame = lax.axis_index("frame")
    for slot, (distance, shifted) in enumerate(EXCHANGES):
        offset, _ = partner(frame, distance, shifted)
        wanted = wanted_ref[slot : slot + 1, :]
        chosen = key_scale[:1]
        for row in range(1, key_scale.shape[0]):
            chosen = jnp.where(wanted == row, key_scale[row : row + 1], chosen)

        @pl.when(is_live(frame, frames, distance, shifted))
        def _():
            scale_ref[frame + offset] = chosen

    row = 0
    for ref, out in ((q_ref, qn_ref), (k_ref, kn_ref)):
        for start in range(0, ref.shape[0], 128):
            factor = by_row(scale[row : row + 1, :])
            row += 1
            for column in range(0, width, 128):
                part = ref[start : start + 128, column : column + 128]
                out[start : start + 128, column : column + 128] = scaled(part, factor)


CONTRACT_LAST = (((1,), (1,)), ((), ()))
CONTRACT_FIRST = (((0,), (0,)), ((), ()))
FACTOR = 1.0 / math.sqrt(HD)
EXPONENT = FACTOR * math.log2(math.e)
CHUNK = 512


def dot(left, right, dims=(((1,), (0,)), ((), ()))):
    return lax.dot_general(left, right, dims, preferred_element_type=jnp.float32)


def attend_kernel(frames, scale_ref, q_ref, k_ref, v_ref, d_ref, *refs):
    far_refs = refs[:5]
    att_ref, w_own, stats, s_far, k_far = refs[5:10]
    back_refs = refs[10:16]
    v_far, p_far = refs[16:]
    frame = lax.axis_index("frame")
    tokens, width = q_ref.shape
    f32 = jnp.float32

    def place(slot, far):
        distance, shifted = EXCHANGES[slot]
        offset, _ = partner(frame, distance, shifted)
        scale = by_row(scale_ref[jnp.clip(frame + offset, 0, frames - 1)])
        start = slot * BS
        for column in range(0, width, 128):
            part = far[:BS, column : column + 128]
            k_far[start : start + BS, column : column + 128] = scaled(part, scale)
        v_far[start : start + BS] = far[:BS, width:]

    for slot, far in zip(FAR_ORDER, far_refs):
        place(slot, far)

    @pl.when(via_near(frame))
    def _():
        place(5, far_refs[1].at[BS:])

    @pl.when(jnp.logical_not(via_near(frame)))
    def _():
        place(5, far_refs[2].at[BS:])

    column = lax.broadcasted_iota(jnp.int32, (1, 6 * BS), 1)
    allowed = column < 0
    for slot, (distance, shifted) in enumerate(EXCHANGES):
        inside = jnp.logical_and(column >= slot * BS, column < (slot + 1) * BS)
        live = is_live(frame, frames, distance, shifted)
        allowed = jnp.logical_or(allowed, jnp.logical_and(inside, live))
    for index in range(width // HD):
        head = slice(index * HD, (index + 1) * HD)
        keys, vals = k_far[:, head], v_far[:, head]
        for first in range(0, tokens, CHUNK):
            rows = slice(first, first + CHUNK)
            grads = d_ref[rows, head]
            own = dot(q_ref[rows, head], k_ref[:, head], CONTRACT_LAST)
            far = jnp.where(allowed, dot(q_ref[rows, head], keys, CONTRACT_LAST), masked_score)
            top = jnp.maximum(jnp.max(own, axis=1, keepdims=True), jnp.max(far, axis=1, keepdims=True))
            own = jnp.exp2((own - top) * EXPONENT)
            w_own[index, rows, :] = own
            far = jnp.exp2((far - top) * EXPONENT)
            share = 1.0 / (jnp.sum(own, axis=1, keepdims=True) + jnp.sum(far, axis=1, keepdims=True))
            own_low = (own * share).astype(jnp.bfloat16)
            far_low = (far * share).astype(jnp.bfloat16)
            p_far[rows, :] = far_low
            attended = (dot(own_low, v_ref[:, head]) + dot(far_low, vals)).astype(jnp.bfloat16)
            att_ref[rows, head] = attended
            inner = jnp.sum(grads.astype(f32) * attended.astype(f32), axis=1, keepdims=True)
            stats[rows, 2 * index : 2 * index + 1] = share
            stats[rows, 2 * index + 1 : 2 * index + 2] = inner
            s_far[index, rows, :] = (far * ((dot(grads, vals, CONTRACT_LAST) - inner) * share)).astype(jnp.bfloat16)
        grad_k = dot(q_ref[:, head].T, s_far[index]).T * FACTOR
        grad_v = dot(d_ref[:, head].T, p_far[...]).T
        for slot, back in zip(RETURN_ORDER, back_refs):
            rows = slice(slot * BS, (slot + 1) * BS)
            back[:, index * HD : (index + 1) * HD] = grad_k[rows].astype(jnp.bfloat16)
            back[:, width + index * HD : width + (index + 1) * HD] = grad_v[rows].astype(jnp.bfloat16)


def rest_kernel(w_own, stats, s_far, k_far, q_ref, k_ref, v_ref, d_ref, gq_ref, gk_ref, gv_ref):
    for index in range(q_ref.shape[1] // HD):
        head = slice(index * HD, (index + 1) * HD)
        share = stats[:, 2 * index : 2 * index + 1]
        inner = stats[:, 2 * index + 1 : 2 * index + 2]
        weights = w_own[index]
        probs = (weights * share).astype(jnp.bfloat16)
        dprobs = dot(d_ref[:, head], v_ref[:, head], CONTRACT_LAST)
        dscores = (weights * ((dprobs - inner) * share)).astype(jnp.bfloat16)
        grad_q = dot(dscores, k_ref[:, head]) + dot(s_far[index], k_far[:, head])
        gq_ref[:, head] = (grad_q * FACTOR).astype(jnp.bfloat16)
        gk_ref[:, head] = dot(dscores, q_ref[:, head], CONTRACT_FIRST) * FACTOR
        gv_ref[:, head] = dot(probs, d_ref[:, head], CONTRACT_FIRST)


def collect_kernel(frames, kept_ref, gk_ref, gv_ref, *refs):
    back_refs, (outk_ref, outv_ref, acc_k, acc_v) = refs[:6], refs[6:]
    frame = lax.axis_index("frame")
    width = gk_ref.shape[1]
    acc_k[...] = gk_ref[...]
    acc_v[...] = gv_ref[...]
    for which, back in zip(RETURN_ORDER, back_refs):
        distance, shifted = EXCHANGES[which]
        rows = pl.ds(block_start(kept_ref, frame, frames, distance, shifted), BS)

        @pl.when(is_live(frame, frames, distance, shifted))
        def _():
            acc_k[rows, :] += back[:, :width].astype(jnp.float32)
            acc_v[rows, :] += back[:, width:].astype(jnp.float32)

    outk_ref[...] = acc_k[...].astype(jnp.bfloat16)
    outv_ref[...] = acc_v[...].astype(jnp.bfloat16)


def exchange(block, frames, which):
    return lax.ppermute(block, "frame", route(*EXCHANGES[which], frames))


def swap_relayed(blocks, frames):
    first, wide_far, near_far, wide_two, near_two = blocks
    got_first = exchange(first, frames, 0)
    got_wide_far = exchange(wide_far, frames, 1)
    got_near_far = exchange(near_far, frames, 2)
    relay = got_first[BS:]
    got_wide_two = exchange(jnp.concatenate([wide_two, relay]), frames, 3)
    got_near_two = exchange(jnp.concatenate([near_two, relay]), frames, 4)
    return got_first, got_near_two, got_wide_two, got_wide_far, got_near_far


def swap(blocks, frames):
    return [exchange(block, frames, which) for which, block in zip(RETURN_ORDER, blocks)]


def on_device(queries, keys, values, cotangent, kept):
    frames = lax.axis_size("frame")
    heads = lax.axis_size("head")
    tokens, width = queries.shape
    kept = kept.T
    stat_rows = 2 * tokens // 128
    flat = jax.ShapeDtypeStruct((tokens, width), jnp.bfloat16)
    wide = jax.ShapeDtypeStruct((tokens, width), jnp.float32)
    block = jax.ShapeDtypeStruct((BS, 2 * width), jnp.bfloat16)
    pair = jax.ShapeDtypeStruct((2 * BS, 2 * width), jnp.bfloat16)
    sums, wanted, *sent = pl.pallas_call(
        functools.partial(prepare_kernel, frames),
        out_shape=[
            jax.ShapeDtypeStruct((heads, stat_rows, 128), jnp.float32),
            jax.ShapeDtypeStruct((8, BS), jnp.int32),
            pair,
        ]
        + [block] * 4,
        in_specs=[SMEM] + [ANY] * 3,
        out_specs=[VMEM] * 7,
        scratch_shapes=[pltpu.VMEM((tokens, width), jnp.bfloat16)] * 3 + [pltpu.SemaphoreType.DMA((3,))],
        compiler_params=params(PREPARE_MIB),
        name="prepare",
    )(kept, queries, keys, values)
    sums = lax.all_to_all(sums, "head", 0, 0)
    far = swap_relayed(sent, frames)
    q_norm, k_norm, scales = pl.pallas_call(
        functools.partial(norm_kernel, frames, width * heads),
        out_shape=[flat, flat, jax.ShapeDtypeStruct((frames, 1, BS), jnp.float32)],
        in_specs=[VMEM] * 4,
        out_specs=[VMEM] * 3,
        compiler_params=params(8),
        name="normalize",
    )(sums, wanted, queries, keys)
    scales = lax.all_to_all(scales, "frame", 0, 0)
    heads_dev = width // HD
    own_shape = (heads_dev, tokens, tokens)
    own_flops = 2 * tokens * tokens * width
    attended, own_w, stats, far_s, far_k, *back = pl.pallas_call(
        functools.partial(attend_kernel, frames),
        out_shape=[
            flat,
            jax.ShapeDtypeStruct(own_shape, jnp.float32),
            jax.ShapeDtypeStruct((tokens, 128), jnp.float32),
            jax.ShapeDtypeStruct((heads_dev, tokens, 6 * BS), jnp.bfloat16),
            jax.ShapeDtypeStruct((6 * BS, width), jnp.bfloat16),
        ]
        + [block] * 6,
        in_specs=[VMEM] * 10,
        out_specs=[VMEM] * 11,
        scratch_shapes=[
            pltpu.VMEM((6 * BS, width), jnp.bfloat16),
            pltpu.VMEM((tokens, 6 * BS), jnp.bfloat16),
        ],
        compiler_params=params(20),
        name="attend",
    )(scales, q_norm, k_norm, values, cotangent, *far)
    grad_q, own_k, own_v = pl.pallas_call(
        rest_kernel,
        out_shape=[flat, wide, wide],
        in_specs=[VMEM] * 8,
        out_specs=[VMEM] * 3,
        compiler_params=params(8),
        cost_estimate=pl.CostEstimate(flops=6 * own_flops, bytes_accessed=8 << 20, transcendentals=0),
        name="rest",
    )(own_w, stats, far_s, far_k, q_norm, k_norm, values, cotangent)
    back = swap(back, frames)
    grad_k, grad_v = pl.pallas_call(
        functools.partial(collect_kernel, frames),
        out_shape=[flat, flat],
        in_specs=[SMEM] + [VMEM] * 8,
        out_specs=[VMEM] * 2,
        scratch_shapes=[pltpu.VMEM((tokens, width), jnp.float32)] * 2,
        compiler_params=params(8),
        name="collect",
    )(kept, own_k, own_v, *back)
    return attended, grad_q, grad_k, grad_v


def solution(mesh):
    spec = P("frame", "head")
    return jax.shard_map(
        on_device,
        mesh=mesh,
        in_specs=(spec, spec, spec, spec, P()),
        out_specs=(spec, spec, spec, spec),
        check_vma=False,
    )
```

```python
import functools
import math

import jax
import jax.numpy as jnp
from jax import lax
from jax.experimental import pallas as pl
from jax.experimental.pallas import tpu as pltpu
from jax.sharding import PartitionSpec as P

HD = 128
BS = 128
EXCHANGES = ((1, False), (4, True), (4, False), (2, True), (2, False), (1, True))
RETURN_ORDER = (1, 3, 5, 2, 4, 0)

masked_score = -1e30
norm_eps = 1e-06

VMEM = pl.BlockSpec(memory_space=pltpu.VMEM)
PREPARE_MIB = 53
ANY = pl.BlockSpec(memory_space=pl.ANY)
SMEM = pl.BlockSpec(memory_space=pltpu.SMEM)


def params(mib):
    return pltpu.CompilerParams(vmem_limit_bytes=mib << 20)


def route(distance, shifted, frames):
    pairs = []
    for low in range(frames - distance):
        if ((low // distance) % 2 == 1) == shifted:
            pairs += [(low, low + distance), (low + distance, low)]
    return pairs


def partner(frame, distance, shifted):
    up = ((frame // distance) % 2 == 1) == shifted
    level = int(math.log2(distance))
    offset = jnp.where(up, distance, -distance)
    slot = jnp.where(up, 2 * level + 1, 2 * level)
    return offset, slot


def block_start(kept_ref, frame, frames, distance, shifted):
    offset, slot = partner(frame, distance, shifted)
    other = jnp.clip(frame + offset, 0, frames - 1)
    return pl.multiple_of(kept_ref[slot, other] * BS, BS)


def is_live(frame, frames, distance, shifted):
    offset, _ = partner(frame, distance, shifted)
    other = frame + offset
    return jnp.logical_and(other >= 0, other < frames)


def via_near(frame):
    return ((frame % 2) ^ ((frame // 2) % 2)) == 1


def prepare_kernel(frames, kept_ref, q_hbm, k_hbm, v_hbm, sums_ref, wanted_ref, *refs):
    block_refs, (q_ref, k_ref, v_ref, sems) = refs[:5], refs[5:]
    copies = [
        pltpu.make_async_copy(source, target, sems.at[index])
        for index, (source, target) in enumerate(((q_hbm, q_ref), (k_hbm, k_ref), (v_hbm, v_ref)))
    ]
    for copy in copies:
        copy.start()
    frame = lax.axis_index("frame")
    width = k_ref.shape[1]
    rows = []
    for copy, ref in zip(copies, (q_ref, k_ref)):
        copy.wait()
        for start in range(0, ref.shape[0], 128):
            total = jnp.zeros((128, 128), jnp.float32)
            for column in range(0, width, 128):
                part = ref[start : start + 128, column : column + 128].astype(jnp.float32)
                total += part * part
            rows.append(jnp.sum(total.T, axis=0, keepdims=True))
    packed = jnp.concatenate(rows, axis=0)
    for copy in range(sums_ref.shape[0]):
        sums_ref[copy] = packed
    wanted = []
    for distance, shifted in EXCHANGES:
        block = block_start(kept_ref, frame, frames, distance, shifted) // BS
        wanted.append(jnp.full((1, BS), block, jnp.int32))
    wanted_ref[...] = jnp.concatenate(wanted + [jnp.zeros((2, BS), jnp.int32)], axis=0)
    copies[2].wait()
    first = block_refs[0]
    targets = [first.at[:BS], *block_refs[1:], first.at[BS:]]
    for (distance, shifted), block in zip(EXCHANGES, targets):
        rows = pl.ds(block_start(kept_ref, frame, frames, distance, shifted), BS)
        block[:, :width] = k_ref[rows, :]
        block[:, width:] = v_ref[rows, :]


def by_row(scale):
    return jnp.broadcast_to(scale, (128, 128)).T


def scaled(block, scale):
    return (block.astype(jnp.float32) * scale).astype(jnp.bfloat16)


def norm_kernel(frames, width_all, sums_ref, wanted_ref, q_ref, k_ref, qn_ref, kn_ref, scale_ref):
    width = q_ref.shape[1]
    total = sums_ref[0]
    for part in range(1, sums_ref.shape[0]):
        total += sums_ref[part]
    scale = lax.rsqrt(total / width_all + norm_eps)
    key_scale = scale[q_ref.shape[0] // 128 :]
    scale_ref[...] = jnp.zeros_like(scale_ref)
    frame = lax.axis_index("frame")
    for slot, (distance, shifted) in enumerate(EXCHANGES):
        offset, _ = partner(frame, distance, shifted)
        wanted = wanted_ref[slot : slot + 1, :]
        chosen = key_scale[:1]
        for row in range(1, key_scale.shape[0]):
            chosen = jnp.where(wanted == row, key_scale[row : row + 1], chosen)

        @pl.when(is_live(frame, frames, distance, shifted))
        def _():
            scale_ref[frame + offset] = chosen

    row = 0
    for ref, out in ((q_ref, qn_ref), (k_ref, kn_ref)):
        for start in range(0, ref.shape[0], 128):
            factor = by_row(scale[row : row + 1, :])
            row += 1
            for column in range(0, width, 128):
                part = ref[start : start + 128, column : column + 128]
                out[start : start + 128, column : column + 128] = scaled(part, factor)


CONTRACT_LAST = (((1,), (1,)), ((), ()))
CONTRACT_FIRST = (((0,), (0,)), ((), ()))
FACTOR = 1.0 / math.sqrt(HD)
EXPONENT = FACTOR * math.log2(math.e)
CHUNK = 512


def dot(left, right, dims=(((1,), (0,)), ((), ()))):
    return lax.dot_general(left, right, dims, preferred_element_type=jnp.float32)


def attend_kernel(frames, scale_ref, q_ref, k_ref, v_ref, d_ref, *refs):
    far_refs = refs[:5]
    att_ref, w_own, stats, s_far, k_far = refs[5:10]
    back_refs = refs[10:16]
    v_far, p_far = refs[16:]
    frame = lax.axis_index("frame")
    tokens, width = q_ref.shape
    f32 = jnp.float32

    def place(slot, far):
        distance, shifted = EXCHANGES[slot]
        offset, _ = partner(frame, distance, shifted)
        scale = by_row(scale_ref[jnp.clip(frame + offset, 0, frames - 1)])
        start = slot * BS
        for column in range(0, width, 128):
            part = far[:BS, column : column + 128]
            k_far[start : start + BS, column : column + 128] = scaled(part, scale)
        v_far[start : start + BS] = far[:BS, width:]

    for slot, far in enumerate(far_refs):
        place(slot, far)

    @pl.when(via_near(frame))
    def _():
        place(5, far_refs[4].at[BS:])

    @pl.when(jnp.logical_not(via_near(frame)))
    def _():
        place(5, far_refs[3].at[BS:])

    column = lax.broadcasted_iota(jnp.int32, (1, 6 * BS), 1)
    allowed = column < 0
    for slot, (distance, shifted) in enumerate(EXCHANGES):
        inside = jnp.logical_and(column >= slot * BS, column < (slot + 1) * BS)
        live = is_live(frame, frames, distance, shifted)
        allowed = jnp.logical_or(allowed, jnp.logical_and(inside, live))
    for index in range(width // HD):
        head = slice(index * HD, (index + 1) * HD)
        keys, vals = k_far[:, head], v_far[:, head]
        for first in range(0, tokens, CHUNK):
            rows = slice(first, first + CHUNK)
            grads = d_ref[rows, head]
            own = dot(q_ref[rows, head], k_ref[:, head], CONTRACT_LAST)
            far = jnp.where(allowed, dot(q_ref[rows, head], keys, CONTRACT_LAST), masked_score)
            top = jnp.maximum(jnp.max(own, axis=1, keepdims=True), jnp.max(far, axis=1, keepdims=True))
            own = jnp.exp2((own - top) * EXPONENT)
            w_own[index, rows, :] = own
            far = jnp.exp2((far - top) * EXPONENT)
            share = 1.0 / (jnp.sum(own, axis=1, keepdims=True) + jnp.sum(far, axis=1, keepdims=True))
            own_low = (own * share).astype(jnp.bfloat16)
            far_low = (far * share).astype(jnp.bfloat16)
            p_far[rows, :] = far_low
            attended = (dot(own_low, v_ref[:, head]) + dot(far_low, vals)).astype(jnp.bfloat16)
            att_ref[rows, head] = attended
            inner = jnp.sum(grads.astype(f32) * attended.astype(f32), axis=1, keepdims=True)
            stats[rows, 2 * index : 2 * index + 1] = share
            stats[rows, 2 * index + 1 : 2 * index + 2] = inner
            s_far[index, rows, :] = (far * ((dot(grads, vals, CONTRACT_LAST) - inner) * share)).astype(jnp.bfloat16)
        grad_k = dot(q_ref[:, head].T, s_far[index]).T * FACTOR
        grad_v = dot(d_ref[:, head].T, p_far[...]).T
        for slot, back in zip(RETURN_ORDER, back_refs):
            rows = slice(slot * BS, (slot + 1) * BS)
            back[:, index * HD : (index + 1) * HD] = grad_k[rows].astype(jnp.bfloat16)
            back[:, width + index * HD : width + (index + 1) * HD] = grad_v[rows].astype(jnp.bfloat16)


def rest_kernel(w_own, stats, s_far, k_far, q_ref, k_ref, v_ref, d_ref, gq_ref, gk_ref, gv_ref):
    for index in range(q_ref.shape[1] // HD):
        head = slice(index * HD, (index + 1) * HD)
        share = stats[:, 2 * index : 2 * index + 1]
        inner = stats[:, 2 * index + 1 : 2 * index + 2]
        weights = w_own[index]
        probs = (weights * share).astype(jnp.bfloat16)
        dprobs = dot(d_ref[:, head], v_ref[:, head], CONTRACT_LAST)
        dscores = (weights * ((dprobs - inner) * share)).astype(jnp.bfloat16)
        grad_q = dot(dscores, k_ref[:, head]) + dot(s_far[index], k_far[:, head])
        gq_ref[:, head] = (grad_q * FACTOR).astype(jnp.bfloat16)
        gk_ref[:, head] = dot(dscores, q_ref[:, head], CONTRACT_FIRST) * FACTOR
        gv_ref[:, head] = dot(probs, d_ref[:, head], CONTRACT_FIRST)


def collect_kernel(frames, kept_ref, gk_ref, gv_ref, *refs):
    back_refs, (outk_ref, outv_ref, acc_k, acc_v) = refs[:6], refs[6:]
    frame = lax.axis_index("frame")
    width = gk_ref.shape[1]
    acc_k[...] = gk_ref[...]
    acc_v[...] = gv_ref[...]
    for which, back in zip(RETURN_ORDER, back_refs):
        distance, shifted = EXCHANGES[which]
        rows = pl.ds(block_start(kept_ref, frame, frames, distance, shifted), BS)

        @pl.when(is_live(frame, frames, distance, shifted))
        def _():
            acc_k[rows, :] += back[:, :width].astype(jnp.float32)
            acc_v[rows, :] += back[:, width:].astype(jnp.float32)

    outk_ref[...] = acc_k[...].astype(jnp.bfloat16)
    outv_ref[...] = acc_v[...].astype(jnp.bfloat16)


def exchange(block, frames, which):
    return lax.ppermute(block, "frame", route(*EXCHANGES[which], frames))


def swap_relayed(blocks, frames):
    first, wide_far, near_far, wide_two, near_two = blocks
    got_first = exchange(first, frames, 0)
    got_wide_far = exchange(wide_far, frames, 1)
    got_near_far = exchange(near_far, frames, 2)
    relay = got_first[BS:]
    got_wide_two = exchange(jnp.concatenate([wide_two, relay]), frames, 3)
    got_near_two = exchange(jnp.concatenate([near_two, relay]), frames, 4)
    return got_first, got_wide_far, got_near_far, got_wide_two, got_near_two


def swap(blocks, frames):
    return [exchange(block, frames, which) for which, block in zip(RETURN_ORDER, blocks)]


def on_device(queries, keys, values, cotangent, kept):
    frames = lax.axis_size("frame")
    heads = lax.axis_size("head")
    tokens, width = queries.shape
    kept = kept.T
    stat_rows = 2 * tokens // 128
    flat = jax.ShapeDtypeStruct((tokens, width), jnp.bfloat16)
    wide = jax.ShapeDtypeStruct((tokens, width), jnp.float32)
    block = jax.ShapeDtypeStruct((BS, 2 * width), jnp.bfloat16)
    pair = jax.ShapeDtypeStruct((2 * BS, 2 * width), jnp.bfloat16)
    sums, wanted, *sent = pl.pallas_call(
        functools.partial(prepare_kernel, frames),
        out_shape=[
            jax.ShapeDtypeStruct((heads, stat_rows, 128), jnp.float32),
            jax.ShapeDtypeStruct((8, BS), jnp.int32),
            pair,
        ]
        + [block] * 4,
        in_specs=[SMEM] + [ANY] * 3,
        out_specs=[VMEM] * 7,
        scratch_shapes=[pltpu.VMEM((tokens, width), jnp.bfloat16)] * 3 + [pltpu.SemaphoreType.DMA((3,))],
        compiler_params=params(PREPARE_MIB),
        name="prepare",
    )(kept, queries, keys, values)
    sums = lax.all_to_all(sums, "head", 0, 0)
    far = swap_relayed(sent, frames)
    q_norm, k_norm, scales = pl.pallas_call(
        functools.partial(norm_kernel, frames, width * heads),
        out_shape=[flat, flat, jax.ShapeDtypeStruct((frames, 1, BS), jnp.float32)],
        in_specs=[VMEM] * 4,
        out_specs=[VMEM] * 3,
        compiler_params=params(8),
        name="normalize",
    )(sums, wanted, queries, keys)
    scales = lax.all_to_all(scales, "frame", 0, 0)
    heads_dev = width // HD
    own_shape = (heads_dev, tokens, tokens)
    own_flops = 2 * tokens * tokens * width
    attended, own_w, stats, far_s, far_k, *back = pl.pallas_call(
        functools.partial(attend_kernel, frames),
        out_shape=[
            flat,
            jax.ShapeDtypeStruct(own_shape, jnp.float32),
            jax.ShapeDtypeStruct((tokens, 128), jnp.float32),
            jax.ShapeDtypeStruct((heads_dev, tokens, 6 * BS), jnp.bfloat16),
            jax.ShapeDtypeStruct((6 * BS, width), jnp.bfloat16),
        ]
        + [block] * 6,
        in_specs=[VMEM] * 10,
        out_specs=[VMEM] * 11,
        scratch_shapes=[
            pltpu.VMEM((6 * BS, width), jnp.bfloat16),
            pltpu.VMEM((tokens, 6 * BS), jnp.bfloat16),
        ],
        compiler_params=params(20),
        name="attend",
    )(scales, q_norm, k_norm, values, cotangent, *far)
    grad_q, own_k, own_v = pl.pallas_call(
        rest_kernel,
        out_shape=[flat, wide, wide],
        in_specs=[VMEM] * 8,
        out_specs=[VMEM] * 3,
        compiler_params=params(8),
        cost_estimate=pl.CostEstimate(flops=6 * own_flops, bytes_accessed=8 << 20, transcendentals=0),
        name="rest",
    )(own_w, stats, far_s, far_k, q_norm, k_norm, values, cotangent)
    back = swap(back, frames)
    grad_k, grad_v = pl.pallas_call(
        functools.partial(collect_kernel, frames),
        out_shape=[flat, flat],
        in_specs=[SMEM] + [VMEM] * 8,
        out_specs=[VMEM] * 2,
        scratch_shapes=[pltpu.VMEM((tokens, width), jnp.float32)] * 2,
        compiler_params=params(8),
        name="collect",
    )(kept, own_k, own_v, *back)
    return attended, grad_q, grad_k, grad_v


def solution(mesh):
    spec = P("frame", "head")
    return jax.shard_map(
        on_device,
        mesh=mesh,
        in_specs=(spec, spec, spec, spec, P()),
        out_specs=(spec, spec, spec, spec),
        check_vma=False,
    )
```
